32 devices in a mesh: grp: 4 (over x, core), seq: 8 (over z, y).
Axes of the slice: x: 2, y: 2, z: 4, core: 2. Of those that a mesh axis runs over, the one named last changes fastest.
Arguments:
- tile_cls: bfloat16 [8192, 1536], P(('grp', 'seq')), may hold values from -6 to 6
- ln_gain: float32 [1536], replicated, may hold values from 0.25 to 1.75
- ln_bias: float32 [1536], replicated, may hold values from -1.5 to 1.5
- gate_weight: bfloat16 [4096, 1536], P('seq'), may hold values from -0.15625 to 0.15625
- up_weight: bfloat16 [4096, 1536], P('seq'), may hold values from -0.15625 to 0.15625
- down_weight: bfloat16 [4096, 1536], P('seq'), may hold values from -0.09375 to 0.09375
- layer_scale: float32 [1536], replicated, may hold values from 0.25 to 1.75
- final_gain: float32 [1536], replicated, may hold values from 0.25 to 1.75
- final_bias: float32 [1536], replicated, may hold values from -1.5 to 1.5
- proj_weight: bfloat16 [1536, 768], replicated, may hold values from -0.15625 to 0.15625
- proj_bias: float32 [768], replicated, may hold values from -1.5 to 1.5
- slot: int32 [8192], P(('grp', 'seq')), may hold values from 0 to 8191, as said below
- slide_lengths: int32 [4, 4], P('grp'), may hold values from 1 to 1024, 2048 in all within a row
- attn_gain: float32 [768], replicated, may hold values from 0.25 to 1.75
- attn_bias: float32 [768], replicated, may hold values from -1.5 to 1.5
- q_weight: bfloat16 [768, 768], replicated
- k_weight: bfloat16 [768, 768], replicated
- v_weight: bfloat16 [768, 768], replicated, may hold values from -0.21875 to 0.21875
- o_weight: bfloat16 [768, 768], replicated, may hold values from -0.21875 to 0.21875
Outputs:
- slide_out: bfloat16 [4, 2048, 768], P('grp', 'seq')
The draws below stay inside these ranges and needn't reach their ends.
Inputs may be any that keep to these rules, and one draw needn't show every extreme that they name: slot is a permutation of all tile positions; tile t goes to device slot[t] // 256 (grp major, then seq), row slot[t] % 256; at most 16 tiles of one device go to one device, and that count is reached. `slide_lengths`: each group's lengths add up to 2048.
All inputs are finite; a program needn't handle non-finite values.
Results may differ from the reference program's by a relative error of at most 0.014.
Values may be sent and summed in bfloat16 or wider, within the bound.
A program may use at most 128 MiB of HBM per device.

```python
import math
import jax
import jax.numpy as jnp
import numpy as np
from jax import lax

D_TILE = 1536
FF = 4096
D = 768
HEADS = 12
HEAD_DIM = 64
W_SEG = 1024
RATE = 16
SLIDES = 4
TILE_DEV = 256
TILES = 8192
SEQ_LEN = 2048
CAP = 16
N_GRP = 4


def draw_slot(key, part):
    devices = TILES // TILE_DEV
    pair_count = TILE_DEV // CAP - 1
    pieces = 1 + 2 * pair_count
    first_key, offset_key, source_key, target_key = jax.random.split(jax.random.fold_in(key, 3), 4)
    first_sizes = jax.random.randint(first_key, (pair_count,), 1, CAP)
    paired = jnp.stack([first_sizes, CAP - first_sizes], 1).reshape(-1)
    sizes = jnp.concatenate([jnp.full((1,), CAP, jnp.int32), paired.astype(jnp.int32)])
    offsets = jax.random.permutation(offset_key, devices)[:pieces].astype(jnp.int32)
    piece_of = jnp.repeat(jnp.arange(pieces, dtype=jnp.int32), sizes, total_repeat_length=TILE_DEV)
    source_perm = jax.vmap(lambda sub_key: jax.random.permutation(sub_key, TILE_DEV))(jax.random.split(source_key, devices)).astype(jnp.int32)
    target_perm = jax.vmap(lambda sub_key: jax.random.permutation(sub_key, TILE_DEV))(jax.random.split(target_key, devices)).astype(jnp.int32)
    source_ids = jnp.arange(devices, dtype=jnp.int32)[:, None]
    target_dev = (source_ids + offsets[piece_of][None, :]) % devices
    column_ids = jnp.broadcast_to(jnp.arange(TILE_DEV, dtype=jnp.int32)[None, :], (devices, TILE_DEV))
    position = target_perm[target_dev, column_ids]
    ordered = target_dev * TILE_DEV + position
    inverse = jnp.argsort(source_perm, axis=1)
    return jnp.take_along_axis(ordered, inverse, axis=1).reshape(-1).astype(jnp.int32)


def shared_base(key):
    return jax.random.normal(jax.random.fold_in(key, 7), (D, D), jnp.float32) * D ** (-0.5)


def draw_k_weight(key, part):
    return shared_base(key).astype(jnp.bfloat16)


def draw_q_weight(key, part):
    fresh = jax.random.normal(jax.random.fold_in(key, 11), (D, D), jnp.float32) * (3.0 * D ** (-0.5))
    return fresh.astype(jnp.bfloat16)


def levels(own_key, extent, cuts, least, largest):
    def one(axis_at, shards_of):
        heights = jax.random.uniform(jax.random.fold_in(jax.random.fold_in(own_key, 6), axis_at), (shards_of,), jnp.float32, least / len(cuts), largest / len(cuts))
        return jnp.repeat(jnp.exp(heights), extent[axis_at] // shards_of).reshape((-1,) + (1,) * (len(extent) - axis_at - 1))

    factor_of = one(*cuts[0])
    for cut in cuts[1:]:
        factor_of = factor_of * one(*cut)
    return factor_of


def length_profile(count, total, bound, lean):
    weights = [(1 << 20) // math.isqrt(grade ** lean) + 1 for grade in range(2, count + 1)]
    spare, holding = total - bound - (count - 1), [1] * (count - 1)
    while spare > 0:
        free = [i for i in range(count - 1) if holding[i] < bound]
        pool, remaining = sum([weights[i] for i in free]), spare
        for i in free:
            more = min(bound - holding[i], max(1, remaining * weights[i] // pool), spare)
            holding[i] = holding[i] + more
            spare = spare - more
    return np.array([bound] + holding)


def uneven_parts(stream_key, number_of, total, reach, lean):
    if number_of == 2:
        one = jax.random.randint(stream_key, (), max(1, total - reach), min(reach, total - 1) + 1)
        return jnp.stack([one, total - one])
    sizes = jnp.asarray(length_profile(number_of, total, reach, lean), jnp.int32)
    couples = (number_of - 1) // 2
    giver, sink = sizes[1:1 + 2 * couples:2], sizes[2:2 + 2 * couples:2]
    slack = jnp.minimum(giver - 1, reach - sink)
    passed = jax.random.randint(jax.random.fold_in(stream_key, 1), (couples,), 0, 1 << 20) % (slack + 1)
    sizes = sizes.at[1:1 + 2 * couples:2].set(giver - passed).at[2:2 + 2 * couples:2].set(sink + passed)
    return sizes[jax.random.permutation(jax.random.fold_in(stream_key, 2), number_of)]


def bell_draw(key, shape, spread, most, cuts=(), kind=jnp.bfloat16):
    factor_of = levels(key, shape, cuts, -0.22, 0.18) if cuts else 1.0
    drawn = jax.random.normal(key, shape, jnp.float32) * spread * factor_of
    return jnp.minimum(jnp.maximum(drawn, -most), most).astype(kind)


def setup_inputs(seed: int = 0) -> dict:
    streams_of = jax.random.split(jax.random.key(seed), 20)
    tile_cls = bell_draw(streams_of[0], (TILES, D_TILE), 1.0, 6.0, ((0, 32),))
    ln_gain = jnp.clip(1.0 + 0.15 * jax.random.normal(streams_of[1], (D_TILE,), jnp.float32), 0.25, 1.75)
    ln_bias = bell_draw(streams_of[2], (D_TILE,), 0.3, 1.5, (), jnp.float32)
    gate_weight = bell_draw(streams_of[3], (FF, D_TILE), D_TILE ** -0.5, 0.15625, ((0, 8),))
    up_weight = bell_draw(streams_of[4], (FF, D_TILE), D_TILE ** -0.5, 0.15625, ((0, 8),))
    down_weight = bell_draw(streams_of[5], (FF, D_TILE), FF ** -0.5, 0.09375, ((0, 8),))
    layer_scale = jnp.clip(1.0 + 0.15 * jax.random.normal(streams_of[6], (D_TILE,), jnp.float32), 0.25, 1.75)
    final_gain = jnp.clip(1.0 + 0.15 * jax.random.normal(streams_of[7], (D_TILE,), jnp.float32), 0.25, 1.75)
    final_bias = bell_draw(streams_of[8], (D_TILE,), 0.3, 1.5, (), jnp.float32)
    proj_weight = bell_draw(streams_of[9], (D_TILE, D), D_TILE ** -0.5, 0.15625)
    proj_bias = bell_draw(streams_of[10], (D,), 0.3, 1.5, (), jnp.float32)
    slot = draw_slot(jax.random.fold_in(streams_of[19], 71), 0)
    slide_lengths = jax.vmap(lambda own: uneven_parts(own, SLIDES, SEQ_LEN, SEQ_LEN // 2, 2))(jax.random.split(streams_of[12], N_GRP)).reshape((N_GRP, SLIDES)).astype(jnp.int32)
    attn_gain = jnp.clip(1.0 + 0.15 * jax.random.normal(streams_of[13], (D,), jnp.float32), 0.25, 1.75)
    attn_bias = bell_draw(streams_of[14], (D,), 0.3, 1.5, (), jnp.float32)
    q_weight = draw_q_weight(jax.random.fold_in(streams_of[19], 71), 0)
    k_weight = draw_k_weight(jax.random.fold_in(streams_of[19], 71), 0)
    v_weight = bell_draw(streams_of[17], (D, D), D ** -0.5, 0.21875)
    o_weight = bell_draw(streams_of[18], (D, D), D ** -0.5, 0.21875)
    return dict(tile_cls=tile_cls, ln_gain=ln_gain, ln_bias=ln_bias, gate_weight=gate_weight, up_weight=up_weight, down_weight=down_weight, layer_scale=layer_scale, final_gain=final_gain, final_bias=final_bias, proj_weight=proj_weight, proj_bias=proj_bias, slot=slot, slide_lengths=slide_lengths, attn_gain=attn_gain, attn_bias=attn_bias, q_weight=q_weight, k_weight=k_weight, v_weight=v_weight, o_weight=o_weight)


def layer_norm(values, gain_vec, bias_vector):
    average = lax.optimization_barrier(jnp.mean(values, -1, keepdims=True))
    centred = values - average
    variance = lax.optimization_barrier(jnp.mean(centred * centred, -1, keepdims=True))
    return centred * lax.rsqrt(variance + 1e-06) * gain_vec + bias_vector

def attend(queries, keys_proj, values_proj, allowed):
    scores = jnp.einsum('hqd,hkd->hqk', queries.astype(jnp.float32), keys_proj.astype(jnp.float32)) * HEAD_DIM ** (-0.5)
    row_max = lax.optimization_barrier(jnp.max(jnp.where(allowed, scores, -1e+30), -1, keepdims=True))
    weights = jnp.where(allowed, jnp.exp(scores - row_max), 0.0)
    denom_sum = lax.optimization_barrier(jnp.sum(weights, -1))
    rounded = lax.optimization_barrier(weights.astype(jnp.bfloat16)).astype(jnp.float32)
    mixed = jnp.einsum('hqk,hkd->hqd', rounded, values_proj.astype(jnp.float32)) / denom_sum[..., None]
    return (mixed, row_max[..., 0] + jnp.log(denom_sum))

def pick_dilated(array, picked):
    grid = array.reshape(picked, RATE, HEADS, HEAD_DIM)[:, :HEADS]
    return jnp.transpose(jnp.diagonal(grid, axis1=1, axis2=2), (0, 2, 1))

def combine(local_out, local_lse, far_out, far_lse, length):
    picked = length // RATE
    chosen = jnp.tile(jnp.arange(RATE)[:, None] == jnp.arange(HEADS)[None, :], (picked, 1))
    distant_output_total = jnp.broadcast_to(jnp.transpose(far_out, (1, 0, 2))[:, None], (picked, RATE, HEADS, HEAD_DIM)).reshape(length, HEADS, HEAD_DIM)
    distant_logsumexp_total = jnp.broadcast_to(jnp.transpose(far_lse)[:, None], (picked, RATE, HEADS)).reshape(length, HEADS)
    peak = jnp.where(chosen, jnp.maximum(local_lse, distant_logsumexp_total), local_lse)
    local_share = jnp.exp(local_lse - peak)
    far_share = jnp.where(chosen, jnp.exp(distant_logsumexp_total - peak), 0.0)
    mixed = (local_share[..., None] * local_out + far_share[..., None] * distant_output_total) / (local_share + far_share)[..., None]
    return mixed.reshape(length, HEADS * HEAD_DIM)

def slide_layer(embed, lengths, attn_gain, attn_bias, q_weight, k_weight, v_weight, o_weight):
    length = embed.shape[0]
    slide_ends = jnp.cumsum(lengths)
    slide_of = lax.optimization_barrier(jnp.sum((jnp.arange(length)[:, None] >= slide_ends[None, :]).astype(jnp.int32), 1))
    residual = embed.astype(jnp.float32)
    normed_seq = layer_norm(residual, attn_gain, attn_bias).astype(jnp.bfloat16)
    queries = jnp.dot(normed_seq, q_weight, preferred_element_type=jnp.float32).astype(jnp.bfloat16)
    keys_proj = jnp.dot(normed_seq, k_weight, preferred_element_type=jnp.float32).astype(jnp.bfloat16)
    values_proj = jnp.dot(normed_seq, v_weight, preferred_element_type=jnp.float32).astype(jnp.bfloat16)
    segments = length // W_SEG

    def by_segment(array):
        return jnp.transpose(array.reshape(segments, W_SEG, HEADS, HEAD_DIM), (0, 2, 1, 3))
    seg_slide = slide_of.reshape(segments, W_SEG)
    allowed = (seg_slide[:, :, None] == seg_slide[:, None, :])[:, None]
    local_out, local_lse = lax.map(lambda trio: attend(trio[0], trio[1], trio[2], trio[3]), (by_segment(queries), by_segment(keys_proj), by_segment(values_proj), allowed))
    local_out = jnp.transpose(local_out, (0, 2, 1, 3)).reshape(length, HEADS, HEAD_DIM)
    local_lse = jnp.transpose(local_lse, (0, 2, 1)).reshape(length, HEADS)
    picked = length // RATE
    selected_query = jnp.transpose(pick_dilated(queries, picked), (1, 0, 2))
    chosen_k = jnp.transpose(pick_dilated(keys_proj, picked), (1, 0, 2))
    chosen_v = jnp.transpose(pick_dilated(values_proj, picked), (1, 0, 2))
    chosen_slide = jnp.transpose(slide_of.reshape(picked, RATE)[:, :HEADS])
    far_allowed = chosen_slide[:, :, None] == chosen_slide[:, None, :]
    far_out, far_lse = attend(selected_query, chosen_k, chosen_v, far_allowed)
    attn = combine(local_out, local_lse, far_out, far_lse, length).astype(jnp.bfloat16)
    return (residual + jnp.dot(attn, o_weight, preferred_element_type=jnp.float32)).astype(jnp.bfloat16)

def reference(tile_cls, ln_gain, ln_bias, gate_weight, up_weight, down_weight, layer_scale, final_gain, final_bias, proj_weight, proj_bias, slot, slide_lengths, attn_gain, attn_bias, q_weight, k_weight, v_weight, o_weight):

    def tile_block(block_rows):
        residual = block_rows.astype(jnp.float32)
        normed = layer_norm(residual, ln_gain, ln_bias).astype(jnp.bfloat16)
        gate = jnp.dot(normed, gate_weight.T, preferred_element_type=jnp.float32)
        up_part = jnp.dot(normed, up_weight.T, preferred_element_type=jnp.float32)
        hidden = (jax.nn.silu(gate) * up_part).astype(jnp.bfloat16)
        mlp_out = jnp.dot(hidden, down_weight, preferred_element_type=jnp.float32)
        tile_out = residual + layer_scale * mlp_out
        final = layer_norm(tile_out, final_gain, final_bias).astype(jnp.bfloat16)
        return (jnp.dot(final, proj_weight, preferred_element_type=jnp.float32) + proj_bias).astype(jnp.bfloat16)
    embed = lax.map(tile_block, tile_cls.reshape(-1, TILE_DEV, D_TILE)).reshape(TILES, D)
    placed = jnp.zeros((TILES, D), jnp.bfloat16).at[slot].set(embed).reshape(N_GRP, SEQ_LEN, D)

    def one_group(group_pair):
        return slide_layer(group_pair[0], group_pair[1], attn_gain, attn_bias, q_weight, k_weight, v_weight, o_weight)
    return lax.map(one_group, (placed, slide_lengths))
```

```python
import jax
import jax.numpy as jnp
from jax import lax
from jax.sharding import PartitionSpec as P

HEADS = 12
HEAD_DIM = 64
W_SEG = 1024
RATE = 16


def crossed(block, offset):
    count = lax.axis_size("seq")
    return lax.ppermute(block, "seq", [(low, low ^ offset) for low in range(count)])


def z_shape():
    count = lax.axis_size("seq")
    depth = min(4, count)
    return depth, count // depth


def z_hop(block, step, senders):
    _, across = z_shape()
    route = [(z * across + y, (z + step) * across + y) for z in senders for y in range(across)]
    return lax.ppermute(block, "seq", route)


def z_slots(block, z_index):
    depth, _ = z_shape()
    right, left = block, block
    rights, lefts = {}, {}
    for k in range(1, depth):
        right = z_hop(right, 1, range(k - 1, depth - 1))
        left = z_hop(left, -1, range(1, depth - k + 1))
        rights[k], lefts[k] = right, left
    return [block] + [
        jnp.where(z_index >= k, rights[k], lefts[depth - k]) for k in range(1, depth)
    ]


def z_reduce(parts):
    depth, _ = z_shape()
    right = left = None
    for t in range(1, depth):
        to_right, to_left = parts[t], parts[depth - t]
        if right is not None:
            to_right, to_left = to_right + right, to_left + left
        right = z_hop(to_right.astype(jnp.bfloat16), 1, range(t)).astype(jnp.float32)
        left = z_hop(to_left.astype(jnp.bfloat16), -1, range(depth - t, depth)).astype(
            jnp.float32
        )
    return parts[0] if right is None else parts[0] + right + left


def y_weights(weights):
    _, across = z_shape()
    half = weights[0].shape[0] // 2
    first = lax.axis_index("grp") % 2 * half
    twins = [(low, low ^ 1) for low in range(lax.axis_size("grp"))]
    out = []
    for weight in weights:
        mine = lax.dynamic_slice_in_dim(weight, first, half, 0)
        pieces = []
        for offset in range(1, across):
            piece = crossed(mine, offset)
            pieces += [piece, lax.ppermute(piece, "grp", twins)]
        out.append(jnp.concatenate(pieces, 0) if pieces else None)
    return out


def layer_norm(values, gain_vec, bias_vector):
    average = jnp.mean(values, -1, keepdims=True)
    centred = values - average
    variance = jnp.mean(centred * centred, -1, keepdims=True)
    return centred * lax.rsqrt(variance + 1e-06) * gain_vec + bias_vector


def swiglu_term(normed_rows, gate_rows, up_rows, down_rows):
    dims = (((1,), (1,)), ((), ()))
    gate = lax.dot_general(normed_rows, gate_rows, dims, preferred_element_type=jnp.float32)
    up_part = lax.dot_general(normed_rows, up_rows, dims, preferred_element_type=jnp.float32)
    hidden = (jax.nn.silu(gate) * up_part).astype(jnp.bfloat16)
    return jnp.dot(hidden, down_rows, preferred_element_type=jnp.float32)


def pick_dilated(array):
    width = array.shape[1]
    grid = array.reshape(-1, RATE, width)
    own = jnp.arange(RATE)[:, None] == jnp.arange(width)[None, :] // HEAD_DIM
    return jnp.sum(jnp.where(own[None], grid, 0), 1, dtype=jnp.float32).astype(array.dtype)


def combine(local_out, local_lse, far_out, far_lse, length):
    picked = length // RATE
    chosen = jnp.tile(jnp.arange(RATE)[:, None] == jnp.arange(HEADS)[None, :], (picked, 1))
    distant_output_total = jnp.broadcast_to(
        jnp.transpose(far_out, (1, 0, 2))[:, None], (picked, RATE, HEADS, HEAD_DIM)
    ).reshape(length, HEADS, HEAD_DIM)
    distant_logsumexp_total = jnp.broadcast_to(
        jnp.transpose(far_lse)[:, None], (picked, RATE, HEADS)
    ).reshape(length, HEADS)
    peak = jnp.where(chosen, jnp.maximum(local_lse, distant_logsumexp_total), local_lse)
    local_share = jnp.exp(local_lse - peak)
    far_share = jnp.where(chosen, jnp.exp(distant_logsumexp_total - peak), 0.0)
    mixed = (local_share[..., None] * local_out + far_share[..., None] * distant_output_total) / (
        local_share + far_share
    )[..., None]
    return mixed.reshape(length, HEADS * HEAD_DIM)


def local(
    tile_cls,
    ln_gain,
    ln_bias,
    gate_weight,
    up_weight,
    down_weight,
    layer_scale,
    final_gain,
    final_bias,
    proj_weight,
    proj_bias,
    slot,
    slide_lengths,
    attn_gain,
    attn_bias,
    q_weight,
    k_weight,
    v_weight,
    o_weight,
):
    tile_rows = tile_cls.shape[0]
    width = proj_weight.shape[1]
    residual = tile_cls.astype(jnp.float32)
    normed = layer_norm(residual, ln_gain, ln_bias).astype(jnp.bfloat16)
    seq_index = lax.axis_index("seq")
    _, across = z_shape()
    far_gate, far_up, far_down = y_weights((gate_weight, up_weight, down_weight))
    terms = []
    for rows in z_slots(normed, seq_index // across):
        term = swiglu_term(rows, gate_weight, up_weight, down_weight)
        if across > 1:
            term = term + swiglu_term(rows, far_gate, far_up, far_down)
        terms.append(term)
    mlp_out = z_reduce(terms)
    tile_out = residual + layer_scale * mlp_out
    final = layer_norm(tile_out, final_gain, final_bias).astype(jnp.bfloat16)
    embed = (jnp.dot(final, proj_weight, preferred_element_type=jnp.float32) + proj_bias).astype(
        jnp.bfloat16
    )
    devices = lax.axis_size("grp") * lax.axis_size("seq")
    capacity = 2 * tile_rows // devices
    target = slot // tile_rows
    position = slot % tile_rows
    order = jnp.arange(tile_rows, dtype=jnp.int32)
    same = (target[:, None] == target[None, :]) & (order[None, :] < order[:, None])
    bucket = target * capacity + jnp.sum(same.astype(jnp.int32), 1)
    places = jnp.arange(devices * capacity, dtype=jnp.int32)
    sends = places[:, None] == bucket[None, :]
    outgoing_place = (
        jnp.sum(jnp.where(sends, position[None, :] - tile_rows, 0), 1) + tile_rows
    ).reshape(devices, capacity)
    outgoing = (
        jnp.dot(sends.astype(jnp.bfloat16), embed, preferred_element_type=jnp.float32)
        .astype(jnp.bfloat16)
        .reshape(devices, capacity, width)
    )
    incoming, incoming_place = (
        lax.all_to_all(outgoing, ("grp", "seq"), split_axis=0, concat_axis=0, tiled=True),
        lax.all_to_all(outgoing_place, ("grp", "seq"), split_axis=0, concat_axis=0, tiled=True),
    )
    arrived = incoming.reshape(-1, width)
    arrived_place = incoming_place.reshape(-1)
    lands = (order[:, None] == arrived_place[None, :]).astype(jnp.bfloat16)
    placed = jnp.dot(lands, arrived, preferred_element_type=jnp.float32).astype(jnp.bfloat16)
    start_pos = seq_index * tile_rows
    slide_ends = jnp.cumsum(slide_lengths[0])

    def slides_from(first_pos, count):
        spots = first_pos + jnp.arange(count, dtype=jnp.int32)
        return jnp.sum((spots[:, None] >= slide_ends[None, :]).astype(jnp.int32), 1)

    slide_of = slides_from(start_pos, tile_rows)
    seq_resid = placed.astype(jnp.float32)
    span = W_SEG // tile_rows
    block = jnp.concatenate([placed] + [crossed(placed, r) for r in range(1, span)], 0)
    normed_seq = layer_norm(block.astype(jnp.float32), attn_gain, attn_bias).astype(jnp.bfloat16)
    queries = jnp.dot(
        normed_seq[:tile_rows], q_weight, preferred_element_type=jnp.float32
    ).astype(jnp.bfloat16)
    keys_proj = jnp.dot(normed_seq, k_weight, preferred_element_type=jnp.float32).astype(
        jnp.bfloat16
    )
    values_proj = jnp.dot(normed_seq, v_weight, preferred_element_type=jnp.float32).astype(
        jnp.bfloat16
    )
    scale_factor = HEAD_DIM ** (-0.5)
    chosen = jnp.concatenate([pick_dilated(keys_proj), pick_dilated(values_proj)], 1)
    far_pieces = [chosen] + [
        crossed(chosen, r) for r in range(span, lax.axis_size("seq"), span)
    ]
    head_q = queries.reshape(tile_rows, HEADS, HEAD_DIM)
    key_total = span * tile_rows
    all_keys = keys_proj.reshape(key_total, HEADS, HEAD_DIM)
    all_values = values_proj.reshape(key_total, HEADS, HEAD_DIM)
    key_slides = jnp.concatenate(
        [slides_from((seq_index ^ r) * tile_rows, tile_rows) for r in range(span)]
    )
    all_mask = (slide_of[:, None] == key_slides[None, :])[None]
    scores = (
        jnp.einsum("qhd,khd->hqk", head_q, all_keys, preferred_element_type=jnp.float32)
        * scale_factor
    )
    row_max = jnp.max(jnp.where(all_mask, scores, -1e30), -1, keepdims=True)
    weights = jnp.where(all_mask, jnp.exp(scores - row_max), 0.0)
    denom_sum = jnp.sum(weights, -1)
    mixed = (
        jnp.einsum(
            "hqk,khd->hqd",
            weights.astype(jnp.bfloat16),
            all_values,
            preferred_element_type=jnp.float32,
        )
        / denom_sum[..., None]
    )
    block_lse = row_max[..., 0] + jnp.log(denom_sum)
    local_out = jnp.transpose(mixed, (1, 0, 2))
    local_lse = jnp.transpose(block_lse)
    picked = tile_rows // RATE
    selected_query = pick_dilated(queries).reshape(picked, HEADS, HEAD_DIM)
    query_slide = jnp.transpose(slide_of.reshape(picked, RATE)[:, :HEADS])
    far_rows = jnp.concatenate(far_pieces, 0)
    key_count = far_rows.shape[0]
    key_head_rows = far_rows[:, :width].reshape(key_count, HEADS, HEAD_DIM)
    value_heads = far_rows[:, width:].reshape(key_count, HEADS, HEAD_DIM)
    far_scores = (
        jnp.einsum(
            "tbx,pbx->btp", selected_query, key_head_rows, preferred_element_type=jnp.float32
        )
        * scale_factor
    )
    key_first = jnp.concatenate(
        [
            (seq_index ^ r) * tile_rows + RATE * jnp.arange(picked, dtype=jnp.int32)
            for r in range(lax.axis_size("seq"))
        ]
    )
    key_pos = key_first[None, :] + jnp.arange(HEADS, dtype=jnp.int32)[:, None]
    far_allowed = (
        query_slide[:, :, None]
        == jnp.sum((key_pos[..., None] >= slide_ends[None, None, :]).astype(jnp.int32), -1)[
            :, None, :
        ]
    )
    far_max = jnp.max(jnp.where(far_allowed, far_scores, -1e30), -1, keepdims=True)
    far_weights = jnp.where(far_allowed, jnp.exp(far_scores - far_max), 0.0)
    far_sum = jnp.sum(far_weights, -1)
    far_out = (
        jnp.einsum(
            "gbr,rga->gba",
            far_weights.astype(jnp.bfloat16),
            value_heads,
            preferred_element_type=jnp.float32,
        )
        / far_sum[..., None]
    )
    far_lse = far_max[..., 0] + jnp.log(far_sum)
    attn = combine(local_out, local_lse, far_out, far_lse, tile_rows).astype(jnp.bfloat16)
    result = (seq_resid + jnp.dot(attn, o_weight, preferred_element_type=jnp.float32)).astype(
        jnp.bfloat16
    )
    return result[None]


def solution(mesh):
    return jax.shard_map(
        local,
        mesh=mesh,
        in_specs=(
            P(("grp", "seq"), None),
            P(),
            P(),
            P("seq", None),
            P("seq", None),
            P("seq", None),
            P(),
            P(),
            P(),
            P(),
            P(),
            P(("grp", "seq")),
            P("grp", None),
            P(),
            P(),
            P(),
            P(),
            P(),
            P(),
        ),
        out_specs=P("grp", "seq", None),
        check_vma=False,
    )
```

```python
import functools

import jax
import jax.numpy as jnp
from jax import lax
from jax.experimental import pallas as pl
from jax.experimental.pallas import tpu as pltpu
from jax.sharding import PartitionSpec as P

HEADS = 12
HEAD_DIM = 64
W_SEG = 1024
RATE = 16


def crossed(block, offset):
    count = lax.axis_size("seq")
    return lax.ppermute(block, "seq", [(low, low ^ offset) for low in range(count)])


DEPTH = 4
SPOT = {1: 0, 3: 1, 2: 2, 0: 3}


def ffn_kernel(
    across,
    normed_ref,
    gate_ref,
    up_ref,
    down_ref,
    out_ref,
    tiles,
    weights,
    sums,
    right_out,
    left_out,
    right_in,
    left_in,
    local_sem,
    tile_send,
    tile_recv,
    y_send,
    y_recv,
    twin_send,
    twin_recv,
    right_send,
    right_recv,
    left_send,
    left_recv,
):
    seq = lax.axis_index("seq")
    grp = lax.axis_index("grp")
    z = seq // across
    y = seq % across
    core = grp % 2
    twin = grp + 1 - 2 * core
    has_right = z < DEPTH - 1
    has_left = z > 0
    rows = out_ref.shape[0]
    count = gate_ref.shape[0]
    half = count // 2
    own = (gate_ref, up_ref, down_ref)

    def y_peer(r):
        return {"seq": z * across + (y + r) % across}

    barrier = pltpu.get_barrier_semaphore()

    @pl.when(has_right)
    def _():
        pl.semaphore_signal(barrier, inc=1, device_id={"seq": seq + across})

    @pl.when(has_left)
    def _():
        pl.semaphore_signal(barrier, inc=1, device_id={"seq": seq - across})

    for r in range(1, across):
        pl.semaphore_signal(barrier, inc=1, device_id=y_peer(r))
    pl.semaphore_signal(barrier, inc=1, device_id={"grp": twin})

    loads = [pltpu.make_async_copy(normed_ref, tiles.at[SPOT[0]], local_sem.at[3])]
    loads += [
        pltpu.make_async_copy(own[i], weights.at[0, i], local_sem.at[i]) for i in range(3)
    ]
    for load in loads:
        load.start()
    pl.semaphore_wait(
        barrier,
        across + has_right.astype(jnp.int32) + has_left.astype(jnp.int32),
    )
    loads[0].wait()

    def hop_right(k):
        return pltpu.make_async_remote_copy(
            src_ref=tiles.at[SPOT[k - 1]],
            dst_ref=tiles.at[SPOT[k]],
            send_sem=tile_send.at[0, k - 1],
            recv_sem=tile_recv.at[k - 1],
            device_id={"seq": seq + across},
        )

    def hop_left(k):
        return pltpu.make_async_remote_copy(
            src_ref=tiles.at[SPOT[(DEPTH - k + 1) % DEPTH]],
            dst_ref=tiles.at[SPOT[DEPTH - k]],
            send_sem=tile_send.at[1, k - 1],
            recv_sem=tile_recv.at[DEPTH - k - 1],
            device_id={"seq": seq - across},
        )

    mine = pl.ds(pl.multiple_of(core * half, half), half)
    theirs = pl.ds(pl.multiple_of((1 - core) * half, half), half)

    def y_copy(r, i):
        return pltpu.make_async_remote_copy(
            src_ref=own[i].at[mine],
            dst_ref=weights.at[r, i, mine],
            send_sem=y_send.at[r, i],
            recv_sem=y_recv.at[r, i],
            device_id=y_peer(r),
        )

    def twin_copy(r, i, part):
        return pltpu.make_async_remote_copy(
            src_ref=weights.at[r, i, part],
            dst_ref=weights.at[r, i, part],
            send_sem=twin_send.at[r, i],
            recv_sem=twin_recv.at[r, i],
            device_id={"grp": twin},
        )

    @pl.when(has_right)
    def _():
        hop_right(1).start()

    @pl.when(has_left)
    def _():
        hop_left(1).start()

    fetches = [(r, i) for r in range(1, across) for i in range(3)]
    for r, i in fetches:
        y_copy(r, i).start()

    def relay(r, i):
        y_copy(r, i).wait_recv()
        twin_copy(r, i, mine).start()

    marks = [len(fetches) // 3, 2 * len(fetches) // 3]
    done = 0
    for k in range(1, DEPTH):

        @pl.when(z >= k)
        def _():
            hop_right(k).wait_recv()

        if k < DEPTH - 1:

            @pl.when((z >= k) & has_right)
            def _():
                hop_right(k + 1).start()

        @pl.when(z <= DEPTH - 1 - k)
        def _():
            hop_left(k).wait_recv()

        if k < DEPTH - 1:

            @pl.when((z <= DEPTH - 1 - k) & has_left)
            def _():
                hop_left(k + 1).start()

            while done < marks[k - 1]:
                relay(*fetches[done])
                done += 1
    while done < len(fetches):
        relay(*fetches[done])
        done += 1
    for load in loads[1:]:
        load.wait()
    for r, i in fetches:
        twin_copy(r, i, theirs).wait_recv()

    def products(first):
        def step(index, carry):
            spot = first + index // across
            r = index % across
            tile = tiles[spot]
            dims = (((1,), (1,)), ((), ()))
            gate = lax.dot_general(
                tile, weights[r, 0], dims, preferred_element_type=jnp.float32
            )
            up_part = lax.dot_general(
                tile, weights[r, 1], dims, preferred_element_type=jnp.float32
            )
            hidden = (gate / (1.0 + jnp.exp(-gate)) * up_part).astype(jnp.bfloat16)
            term = jnp.dot(hidden, weights[r, 2], preferred_element_type=jnp.float32)

            @pl.when(r == 0)
            def _():
                sums[spot] = term

            @pl.when(r > 0)
            def _():
                sums[spot] += term

            return carry

        lax.fori_loop(0, 2 * across, step, 0)

    def sum_right(t):
        return pltpu.make_async_remote_copy(
            src_ref=right_out.at[t - 1],
            dst_ref=right_in.at[t - 1],
            send_sem=right_send.at[t - 1],
            recv_sem=right_recv.at[t - 1],
            device_id={"seq": seq + across},
        )

    def sum_left(t):
        return pltpu.make_async_remote_copy(
            src_ref=left_out.at[t - 1],
            dst_ref=left_in.at[t - 1],
            send_sem=left_send.at[t - 1],
            recv_sem=left_recv.at[t - 1],
            device_id={"seq": seq - across},
        )

    def pass_on(t):
        right_term, left_term = sums.at[SPOT[t]], sums.at[SPOT[DEPTH - t]]

        @pl.when(z == 0)
        def _():
            right_out[t - 1] = right_term[...].astype(jnp.bfloat16)

        @pl.when(z == DEPTH - 1)
        def _():
            left_out[t - 1] = left_term[...].astype(jnp.bfloat16)

        if t > 1:

            @pl.when((z >= 1) & (z <= t - 1))
            def _():
                sum_right(t - 1).wait_recv()
                right_out[t - 1] = (
                    right_term[...] + right_in[t - 2].astype(jnp.float32)
                ).astype(jnp.bfloat16)

        @pl.when((z <= t - 1) & has_right)
        def _():
            sum_right(t).start()

        if t > 1:

            @pl.when((z <= DEPTH - 2) & (z >= DEPTH - t))
            def _():
                sum_left(t - 1).wait_recv()
                left_out[t - 1] = (
                    left_term[...] + left_in[t - 2].astype(jnp.float32)
                ).astype(jnp.bfloat16)

        @pl.when((z >= DEPTH - t) & has_left)
        def _():
            sum_left(t).start()

    products(0)
    pass_on(1)
    products(2)
    pass_on(2)
    pass_on(3)

    @pl.when(has_left)
    def _():
        sum_right(DEPTH - 1).wait_recv()
        sums[SPOT[0]] += right_in[DEPTH - 2].astype(jnp.float32)

    @pl.when(has_right)
    def _():
        sum_left(DEPTH - 1).wait_recv()
        sums[SPOT[0]] += left_in[DEPTH - 2].astype(jnp.float32)

    out_ref[...] = sums[SPOT[0]]

    for k in range(1, DEPTH):

        @pl.when((z >= k - 1) & has_right)
        def _():
            hop_right(k).wait_send()

        @pl.when((z <= DEPTH - k) & has_left)
        def _():
            hop_left(k).wait_send()

        @pl.when((z <= k - 1) & has_right)
        def _():
            sum_right(k).wait_send()

        @pl.when((z >= DEPTH - k) & has_left)
        def _():
            sum_left(k).wait_send()

    for r, i in fetches:
        y_copy(r, i).wait_send()
        twin_copy(r, i, mine).wait_send()


def ffn_sums(normed, gate_weight, up_weight, down_weight):
    across = lax.axis_size("seq") // DEPTH
    rows, width = normed.shape
    count = gate_weight.shape[0]
    messages = pltpu.VMEM((DEPTH - 1, rows, width), jnp.bfloat16)
    sem = pltpu.SemaphoreType.DMA
    flops = 6 * DEPTH * rows * across * count * width
    return pl.pallas_call(
        functools.partial(ffn_kernel, across),
        out_shape=jax.ShapeDtypeStruct((rows, width), jnp.float32),
        in_specs=[pl.BlockSpec(memory_space=pl.ANY)] * 4,
        out_specs=pl.BlockSpec(memory_space=pltpu.VMEM),
        scratch_shapes=[
            pltpu.VMEM((DEPTH, rows, width), jnp.bfloat16),
            pltpu.VMEM((across, 3, count, width), jnp.bfloat16),
            pltpu.VMEM((DEPTH, rows, width), jnp.float32),
            messages,
            messages,
            messages,
            messages,
            sem((4,)),
            sem((2, DEPTH - 1)),
            sem((DEPTH - 1,)),
            sem((across, 3)),
            sem((across, 3)),
            sem((across, 3)),
            sem((across, 3)),
            sem((DEPTH - 1,)),
            sem((DEPTH - 1,)),
            sem((DEPTH - 1,)),
            sem((DEPTH - 1,)),
        ],
        compiler_params=pltpu.CompilerParams(
            collective_id=0, has_side_effects=True, vmem_limit_bytes=48 << 20
        ),
        cost_estimate=pl.CostEstimate(
            flops=flops, bytes_accessed=6 * count * width, transcendentals=0
        ),
    )(normed, gate_weight, up_weight, down_weight)


def layer_norm(values, gain_vec, bias_vector):
    average = jnp.mean(values, -1, keepdims=True)
    centred = values - average
    variance = jnp.mean(centred * centred, -1, keepdims=True)
    return centred * lax.rsqrt(variance + 1e-06) * gain_vec + bias_vector


def pick_dilated(array):
    width = array.shape[1]
    grid = array.reshape(-1, RATE, width)
    own = jnp.arange(RATE)[:, None] == jnp.arange(width)[None, :] // HEAD_DIM
    return jnp.sum(jnp.where(own[None], grid, 0), 1, dtype=jnp.float32).astype(array.dtype)


def combine(local_out, local_lse, far_out, far_lse, length):
    picked = length // RATE
    chosen = jnp.tile(jnp.arange(RATE)[:, None] == jnp.arange(HEADS)[None, :], (picked, 1))
    distant_output_total = jnp.broadcast_to(
        jnp.transpose(far_out, (1, 0, 2))[:, None], (picked, RATE, HEADS, HEAD_DIM)
    ).reshape(length, HEADS, HEAD_DIM)
    distant_logsumexp_total = jnp.broadcast_to(
        jnp.transpose(far_lse)[:, None], (picked, RATE, HEADS)
    ).reshape(length, HEADS)
    peak = jnp.where(chosen, jnp.maximum(local_lse, distant_logsumexp_total), local_lse)
    local_share = jnp.exp(local_lse - peak)
    far_share = jnp.where(chosen, jnp.exp(distant_logsumexp_total - peak), 0.0)
    mixed = (local_share[..., None] * local_out + far_share[..., None] * distant_output_total) / (
        local_share + far_share
    )[..., None]
    return mixed.reshape(length, HEADS * HEAD_DIM)


def local(
    tile_cls,
    ln_gain,
    ln_bias,
    gate_weight,
    up_weight,
    down_weight,
    layer_scale,
    final_gain,
    final_bias,
    proj_weight,
    proj_bias,
    slot,
    slide_lengths,
    attn_gain,
    attn_bias,
    q_weight,
    k_weight,
    v_weight,
    o_weight,
):
    tile_rows = tile_cls.shape[0]
    width = proj_weight.shape[1]
    residual = tile_cls.astype(jnp.float32)
    normed = layer_norm(residual, ln_gain, ln_bias).astype(jnp.bfloat16)
    seq_index = lax.axis_index("seq")
    mlp_out = ffn_sums(normed, gate_weight, up_weight, down_weight)
    tile_out = residual + layer_scale * mlp_out
    final = layer_norm(tile_out, final_gain, final_bias).astype(jnp.bfloat16)
    embed = (jnp.dot(final, proj_weight, preferred_element_type=jnp.float32) + proj_bias).astype(
        jnp.bfloat16
    )
    devices = lax.axis_size("grp") * lax.axis_size("seq")
    capacity = 2 * tile_rows // devices
    target = slot // tile_rows
    position = slot % tile_rows
    order = jnp.arange(tile_rows, dtype=jnp.int32)
    same = (target[:, None] == target[None, :]) & (order[None, :] < order[:, None])
    bucket = target * capacity + jnp.sum(same.astype(jnp.int32), 1)
    places = jnp.arange(devices * capacity, dtype=jnp.int32)
    sends = places[:, None] == bucket[None, :]
    lane = jnp.arange(128, dtype=jnp.int32)[None, :]
    code = jnp.where(lane == 0, position[:, None] // 16, position[:, None] % 16)
    code = jnp.where(lane < 2, code, 0) + (lane == 2)
    tagged = jnp.concatenate([embed, code.astype(jnp.bfloat16)], 1)
    outgoing = (
        jnp.dot(sends.astype(jnp.bfloat16), tagged, preferred_element_type=jnp.float32)
        .astype(jnp.bfloat16)
        .reshape(devices, capacity, width + 128)
    )
    incoming = lax.all_to_all(outgoing, ("grp", "seq"), split_axis=0, concat_axis=0, tiled=True)
    incoming = incoming.reshape(-1, width + 128)
    arrived = incoming[:, :width]
    tags = incoming[:, width : width + 3].astype(jnp.int32)
    arrived_place = jnp.where(tags[:, 2] == 1, tags[:, 0] * 16 + tags[:, 1], tile_rows)
    lands = (order[:, None] == arrived_place[None, :]).astype(jnp.bfloat16)
    placed = jnp.dot(lands, arrived, preferred_element_type=jnp.float32).astype(jnp.bfloat16)
    start_pos = seq_index * tile_rows
    slide_ends = jnp.cumsum(slide_lengths[0])

    def slides_from(first_pos, count):
        spots = first_pos + jnp.arange(count, dtype=jnp.int32)
        return jnp.sum((spots[:, None] >= slide_ends[None, :]).astype(jnp.int32), 1)

    slide_of = slides_from(start_pos, tile_rows)
    seq_resid = placed.astype(jnp.float32)
    span = W_SEG // tile_rows
    block = jnp.concatenate([placed] + [crossed(placed, r) for r in range(1, span)], 0)
    normed_seq = layer_norm(block.astype(jnp.float32), attn_gain, attn_bias).astype(jnp.bfloat16)
    queries = jnp.dot(
        normed_seq[:tile_rows], q_weight, preferred_element_type=jnp.float32
    ).astype(jnp.bfloat16)
    keys_proj = jnp.dot(normed_seq, k_weight, preferred_element_type=jnp.float32).astype(
        jnp.bfloat16
    )
    values_proj = jnp.dot(normed_seq, v_weight, preferred_element_type=jnp.float32).astype(
        jnp.bfloat16
    )
    scale_factor = HEAD_DIM ** (-0.5)
    chosen = jnp.concatenate([pick_dilated(keys_proj), pick_dilated(values_proj)], 1)
    far_pieces = [chosen] + [
        crossed(chosen, r) for r in range(span, lax.axis_size("seq"), span)
    ]
    head_q = queries.reshape(tile_rows, HEADS, HEAD_DIM)
    key_total = span * tile_rows
    all_keys = keys_proj.reshape(key_total, HEADS, HEAD_DIM)
    all_values = values_proj.reshape(key_total, HEADS, HEAD_DIM)
    key_slides = jnp.concatenate(
        [slides_from((seq_index ^ r) * tile_rows, tile_rows) for r in range(span)]
    )
    all_mask = (slide_of[:, None] == key_slides[None, :])[None]
    scores = (
        jnp.einsum("qhd,khd->hqk", head_q, all_keys, preferred_element_type=jnp.float32)
        * scale_factor
    )
    row_max = jnp.max(jnp.where(all_mask, scores, -1e30), -1, keepdims=True)
    weights = jnp.where(all_mask, jnp.exp(scores - row_max), 0.0)
    denom_sum = jnp.sum(weights, -1)
    mixed = (
        jnp.einsum(
            "hqk,khd->hqd",
            weights.astype(jnp.bfloat16),
            all_values,
            preferred_element_type=jnp.float32,
        )
        / denom_sum[..., None]
    )
    block_lse = row_max[..., 0] + jnp.log(denom_sum)
    local_out = jnp.transpose(mixed, (1, 0, 2))
    local_lse = jnp.transpose(block_lse)
    picked = tile_rows // RATE
    selected_query = pick_dilated(queries).reshape(picked, HEADS, HEAD_DIM)
    query_slide = jnp.transpose(slide_of.reshape(picked, RATE)[:, :HEADS])
    far_rows = jnp.concatenate(far_pieces, 0)
    key_count = far_rows.shape[0]
    key_head_rows = far_rows[:, :width].reshape(key_count, HEADS, HEAD_DIM)
    value_heads = far_rows[:, width:].reshape(key_count, HEADS, HEAD_DIM)
    far_scores = (
        jnp.einsum(
            "tbx,pbx->btp", selected_query, key_head_rows, preferred_element_type=jnp.float32
        )
        * scale_factor
    )
    key_first = jnp.concatenate(
        [
            (seq_index ^ r) * tile_rows + RATE * jnp.arange(picked, dtype=jnp.int32)
            for r in range(lax.axis_size("seq"))
        ]
    )
    key_pos = key_first[None, :] + jnp.arange(HEADS, dtype=jnp.int32)[:, None]
    far_allowed = (
        query_slide[:, :, None]
        == jnp.sum((key_pos[..., None] >= slide_ends[None, None, :]).astype(jnp.int32), -1)[
            :, None, :
        ]
    )
    far_max = jnp.max(jnp.where(far_allowed, far_scores, -1e30), -1, keepdims=True)
    far_weights = jnp.where(far_allowed, jnp.exp(far_scores - far_max), 0.0)
    far_sum = jnp.sum(far_weights, -1)
    far_out = (
        jnp.einsum(
            "gbr,rga->gba",
            far_weights.astype(jnp.bfloat16),
            value_heads,
            preferred_element_type=jnp.float32,
        )
        / far_sum[..., None]
    )
    far_lse = far_max[..., 0] + jnp.log(far_sum)
    attn = combine(local_out, local_lse, far_out, far_lse, tile_rows).astype(jnp.bfloat16)
    result = (seq_resid + jnp.dot(attn, o_weight, preferred_element_type=jnp.float32)).astype(
        jnp.bfloat16
    )
    return result[None]


def solution(mesh):
    return jax.shard_map(
        local,
        mesh=mesh,
        in_specs=(
            P(("grp", "seq"), None),
            P(),
            P(),
            P("seq", None),
            P("seq", None),
            P("seq", None),
            P(),
            P(),
            P(),
            P(),
            P(),
            P(("grp", "seq")),
            P("grp", None),
            P(),
            P(),
            P(),
            P(),
            P(),
            P(),
        ),
        out_specs=P("grp", "seq", None),
        check_vma=False,
    )
```

```python
import functools

import jax
import jax.numpy as jnp
from jax import lax
from jax.experimental import pallas as pl
from jax.experimental.pallas import tpu as pltpu
from jax.sharding import PartitionSpec as P

HEADS = 12
HEAD_DIM = 64
W_SEG = 1024
RATE = 16


def crossed(block, offset):
    count = lax.axis_size("seq")
    return lax.ppermute(block, "seq", [(low, low ^ offset) for low in range(count)])


DEPTH = 4
SPOT = {1: 0, 3: 1, 2: 2, 0: 3}


def ffn_kernel(
    across,
    normed_ref,
    gate_ref,
    up_ref,
    down_ref,
    out_ref,
    tiles,
    weights,
    sums,
    right_out,
    left_out,
    right_in,
    left_in,
    local_sem,
    tile_send,
    tile_recv,
    y_send,
    y_recv,
    twin_send,
    twin_recv,
    right_send,
    right_recv,
    left_send,
    left_recv,
):
    seq = lax.axis_index("seq")
    grp = lax.axis_index("grp")
    z = seq // across
    y = seq % across
    core = grp % 2
    twin = grp + 1 - 2 * core
    has_right = z < DEPTH - 1
    has_left = z > 0
    rows = out_ref.shape[0]
    count = gate_ref.shape[0]
    half = count // 2
    own = (gate_ref, up_ref, down_ref)

    def y_peer(r):
        return {"seq": z * across + (y + r) % across}

    barrier = pltpu.get_barrier_semaphore()

    @pl.when(has_right)
    def _():
        pl.semaphore_signal(barrier, inc=1, device_id={"seq": seq + across})

    @pl.when(has_left)
    def _():
        pl.semaphore_signal(barrier, inc=1, device_id={"seq": seq - across})

    for r in range(1, across):
        pl.semaphore_signal(barrier, inc=1, device_id=y_peer(r))
    pl.semaphore_signal(barrier, inc=1, device_id={"grp": twin})

    loads = [pltpu.make_async_copy(normed_ref, tiles.at[SPOT[0]], local_sem.at[3])]
    loads += [
        pltpu.make_async_copy(own[i], weights.at[0, i], local_sem.at[i]) for i in range(3)
    ]
    for load in loads:
        load.start()
    pl.semaphore_wait(
        barrier,
        across + has_right.astype(jnp.int32) + has_left.astype(jnp.int32),
    )
    loads[0].wait()

    def hop_right(k):
        return pltpu.make_async_remote_copy(
            src_ref=tiles.at[SPOT[k - 1]],
            dst_ref=tiles.at[SPOT[k]],
            send_sem=tile_send.at[0, k - 1],
            recv_sem=tile_recv.at[k - 1],
            device_id={"seq": seq + across},
        )

    def hop_left(k):
        return pltpu.make_async_remote_copy(
            src_ref=tiles.at[SPOT[(DEPTH - k + 1) % DEPTH]],
            dst_ref=tiles.at[SPOT[DEPTH - k]],
            send_sem=tile_send.at[1, k - 1],
            recv_sem=tile_recv.at[DEPTH - k - 1],
            device_id={"seq": seq - across},
        )

    mine = pl.ds(pl.multiple_of(core * half, half), half)
    theirs = pl.ds(pl.multiple_of((1 - core) * half, half), half)

    def y_copy(r, i):
        return pltpu.make_async_remote_copy(
            src_ref=own[i].at[mine],
            dst_ref=weights.at[r, i, mine],
            send_sem=y_send.at[r, i],
            recv_sem=y_recv.at[r, i],
            device_id=y_peer(r),
        )

    def twin_copy(r, i, part):
        return pltpu.make_async_remote_copy(
            src_ref=weights.at[r, i, part],
            dst_ref=weights.at[r, i, part],
            send_sem=twin_send.at[r, i],
            recv_sem=twin_recv.at[r, i],
            device_id={"grp": twin},
        )

    @pl.when(has_right)
    def _():
        hop_right(1).start()

    @pl.when(has_left)
    def _():
        hop_left(1).start()

    fetches = [(r, i) for r in range(1, across) for i in range(3)]
    for r, i in fetches:
        y_copy(r, i).start()

    def relay(r, i):
        y_copy(r, i).wait_recv()
        twin_copy(r, i, mine).start()

    marks = [len(fetches) // 3, 2 * len(fetches) // 3]
    done = 0
    for k in range(1, DEPTH):

        @pl.when(z >= k)
        def _():
            hop_right(k).wait_recv()

        if k < DEPTH - 1:

            @pl.when((z >= k) & has_right)
            def _():
                hop_right(k + 1).start()

        @pl.when(z <= DEPTH - 1 - k)
        def _():
            hop_left(k).wait_recv()

        if k < DEPTH - 1:

            @pl.when((z <= DEPTH - 1 - k) & has_left)
            def _():
                hop_left(k + 1).start()

            while done < marks[k - 1]:
                relay(*fetches[done])
                done += 1
    while done < len(fetches):
        relay(*fetches[done])
        done += 1
    for load in loads[1:]:
        load.wait()
    for r, i in fetches:
        twin_copy(r, i, theirs).wait_recv()

    def products(first):
        def step(index, carry):
            spot = first + index // across
            r = index % across
            tile = tiles[spot]
            dims = (((1,), (1,)), ((), ()))
            gate = lax.dot_general(
                tile, weights[r, 0], dims, preferred_element_type=jnp.float32
            )
            up_part = lax.dot_general(
                tile, weights[r, 1], dims, preferred_element_type=jnp.float32
            )
            hidden = (gate / (1.0 + jnp.exp(-gate)) * up_part).astype(jnp.bfloat16)
            term = jnp.dot(hidden, weights[r, 2], preferred_element_type=jnp.float32)

            @pl.when(r == 0)
            def _():
                sums[spot] = term

            @pl.when(r > 0)
            def _():
                sums[spot] += term

            return carry

        lax.fori_loop(0, 2 * across, step, 0)

    def sum_right(t):
        return pltpu.make_async_remote_copy(
            src_ref=right_out.at[t - 1],
            dst_ref=right_in.at[t - 1],
            send_sem=right_send.at[t - 1],
            recv_sem=right_recv.at[t - 1],
            device_id={"seq": seq + across},
        )

    def sum_left(t):
        return pltpu.make_async_remote_copy(
            src_ref=left_out.at[t - 1],
            dst_ref=left_in.at[t - 1],
            send_sem=left_send.at[t - 1],
            recv_sem=left_recv.at[t - 1],
            device_id={"seq": seq - across},
        )

    def pass_on(t):
        right_term, left_term = sums.at[SPOT[t]], sums.at[SPOT[DEPTH - t]]

        @pl.when(z == 0)
        def _():
            right_out[t - 1] = right_term[...].astype(jnp.bfloat16)

        @pl.when(z == DEPTH - 1)
        def _():
            left_out[t - 1] = left_term[...].astype(jnp.bfloat16)

        if t > 1:

            @pl.when((z >= 1) & (z <= t - 1))
            def _():
                sum_right(t - 1).wait_recv()
                right_out[t - 1] = (
                    right_term[...] + right_in[t - 2].astype(jnp.float32)
                ).astype(jnp.bfloat16)

        @pl.when((z <= t - 1) & has_right)
        def _():
            sum_right(t).start()

        if t > 1:

            @pl.when((z <= DEPTH - 2) & (z >= DEPTH - t))
            def _():
                sum_left(t - 1).wait_recv()
                left_out[t - 1] = (
                    left_term[...] + left_in[t - 2].astype(jnp.float32)
                ).astype(jnp.bfloat16)

        @pl.when((z >= DEPTH - t) & has_left)
        def _():
            sum_left(t).start()

    products(0)
    pass_on(1)
    products(2)
    pass_on(2)
    pass_on(3)

    @pl.when(has_left)
    def _():
        sum_right(DEPTH - 1).wait_recv()
        sums[SPOT[0]] += right_in[DEPTH - 2].astype(jnp.float32)

    @pl.when(has_right)
    def _():
        sum_left(DEPTH - 1).wait_recv()
        sums[SPOT[0]] += left_in[DEPTH - 2].astype(jnp.float32)

    out_ref[...] = sums[SPOT[0]]

    for k in range(1, DEPTH):

        @pl.when((z >= k - 1) & has_right)
        def _():
            hop_right(k).wait_send()

        @pl.when((z <= DEPTH - k) & has_left)
        def _():
            hop_left(k).wait_send()

        @pl.when((z <= k - 1) & has_right)
        def _():
            sum_right(k).wait_send()

        @pl.when((z >= DEPTH - k) & has_left)
        def _():
            sum_left(k).wait_send()

    for r, i in fetches:
        y_copy(r, i).wait_send()
        twin_copy(r, i, mine).wait_send()


def ffn_sums(normed, gate_weight, up_weight, down_weight):
    across = lax.axis_size("seq") // DEPTH
    rows, width = normed.shape
    count = gate_weight.shape[0]
    messages = pltpu.VMEM((DEPTH - 1, rows, width), jnp.bfloat16)
    sem = pltpu.SemaphoreType.DMA
    flops = 6 * DEPTH * rows * across * count * width
    return pl.pallas_call(
        functools.partial(ffn_kernel, across),
        out_shape=jax.ShapeDtypeStruct((rows, width), jnp.float32),
        in_specs=[pl.BlockSpec(memory_space=pl.ANY)] * 4,
        out_specs=pl.BlockSpec(memory_space=pltpu.VMEM),
        scratch_shapes=[
            pltpu.VMEM((DEPTH, rows, width), jnp.bfloat16),
            pltpu.VMEM((across, 3, count, width), jnp.bfloat16),
            pltpu.VMEM((DEPTH, rows, width), jnp.float32),
            messages,
            messages,
            messages,
            messages,
            sem((4,)),
            sem((2, DEPTH - 1)),
            sem((DEPTH - 1,)),
            sem((across, 3)),
            sem((across, 3)),
            sem((across, 3)),
            sem((across, 3)),
            sem((DEPTH - 1,)),
            sem((DEPTH - 1,)),
            sem((DEPTH - 1,)),
            sem((DEPTH - 1,)),
        ],
        compiler_params=pltpu.CompilerParams(
            collective_id=0, has_side_effects=True, vmem_limit_bytes=48 << 20
        ),
        cost_estimate=pl.CostEstimate(
            flops=flops, bytes_accessed=6 * count * width, transcendentals=0
        ),
    )(normed, gate_weight, up_weight, down_weight)


def layer_norm(values, gain_vec, bias_vector):
    average = jnp.mean(values, -1, keepdims=True)
    centred = values - average
    variance = jnp.mean(centred * centred, -1, keepdims=True)
    return centred * lax.rsqrt(variance + 1e-06) * gain_vec + bias_vector


def pick_dilated(array):
    width = array.shape[1]
    grid = array.reshape(-1, RATE, width)
    own = jnp.arange(RATE)[:, None] == jnp.arange(width)[None, :] // HEAD_DIM
    return jnp.sum(jnp.where(own[None], grid, 0), 1, dtype=jnp.float32).astype(array.dtype)


def attention_kernel(
    ends_ref,
    query_pos_ref,
    key_pos_ref,
    far_pos_ref,
    query_ref,
    key_ref,
    value_ref,
    far_key_ref,
    far_value_ref,
    o_ref,
    resid_ref,
    out_ref,
    total,
):
    pair = pl.program_id(0)

    def slides(spots):
        return sum((spots >= ends_ref[j]).astype(jnp.int32) for j in range(ends_ref.shape[0]))

    @pl.when(pair == 0)
    def _():
        total[...] = resid_ref[...].astype(jnp.float32)

    query_pos = query_pos_ref[...]
    query_slide = slides(query_pos)
    near = query_slide == slides(key_pos_ref[...])
    query = query_ref[...] * HEAD_DIM ** (-0.5)
    lane = lax.broadcasted_iota(jnp.int32, query.shape, 1)
    dims = (((1,), (1,)), ((), ()))
    results = []
    for which in range(2):
        head = 2 * pair + which
        far = (query_slide == slides(far_pos_ref[...] + head)) & (query_pos % RATE == head)
        masked = jnp.where(lane // HEAD_DIM == which, query, jnp.zeros_like(query))
        scores = lax.dot_general(
            masked, key_ref[...], dims, preferred_element_type=jnp.float32
        )
        far_scores = lax.dot_general(
            masked, far_key_ref[...], dims, preferred_element_type=jnp.float32
        )
        scores = jnp.where(near, scores, -1e30)
        far_scores = jnp.where(far, far_scores, -1e30)
        peak = jnp.maximum(
            jnp.max(scores, -1, keepdims=True), jnp.max(far_scores, -1, keepdims=True)
        )
        share = jnp.exp(scores - peak)
        far_share = jnp.exp(far_scores - peak)
        weight = jnp.sum(share, -1, keepdims=True) + jnp.sum(far_share, -1, keepdims=True)
        mixed = jnp.dot(
            share.astype(jnp.bfloat16), value_ref[...], preferred_element_type=jnp.float32
        ) + jnp.dot(
            far_share.astype(jnp.bfloat16),
            far_value_ref[...],
            preferred_element_type=jnp.float32,
        )
        results.append(mixed / weight)
    attn = jnp.where(lane < HEAD_DIM, results[0], results[1]).astype(jnp.bfloat16)
    total[...] += jnp.dot(attn, o_ref[...], preferred_element_type=jnp.float32)

    @pl.when(pair == pl.num_programs(0) - 1)
    def _():
        out_ref[...] = total[...].astype(jnp.bfloat16)


def attend(ends, query_pos, key_pos, far_pos, queries, keys, values, far_rows, o_weight, placed):
    rows, width = placed.shape
    pairs = width // 128
    key_count, far_count = keys.shape[0], far_rows.shape[0]

    def whole(array):
        return pl.BlockSpec(array.shape, lambda j: (0, 0))

    def column(count, first=0):
        return pl.BlockSpec((count, 128), lambda j: (0, first + j))

    return pl.pallas_call(
        attention_kernel,
        out_shape=jax.ShapeDtypeStruct((rows, width), jnp.bfloat16),
        grid=(pairs,),
        in_specs=[
            pl.BlockSpec(memory_space=pltpu.SMEM),
            whole(query_pos),
            whole(key_pos),
            whole(far_pos),
            column(rows),
            column(key_count),
            column(key_count),
            column(far_count),
            column(far_count, pairs),
            pl.BlockSpec((128, width), lambda j: (j, 0)),
            whole(placed),
        ],
        out_specs=pl.BlockSpec((rows, width), lambda j: (0, 0)),
        scratch_shapes=[pltpu.VMEM((rows, width), jnp.float32)],
        compiler_params=pltpu.CompilerParams(
            dimension_semantics=("arbitrary",), vmem_limit_bytes=32 << 20
        ),
        cost_estimate=pl.CostEstimate(
            flops=8 * rows * (key_count + far_count) * width,
            bytes_accessed=4 * key_count * width,
            transcendentals=rows * (key_count + far_count) * HEADS,
        ),
    )(
        ends,
        query_pos,
        key_pos,
        far_pos,
        queries,
        keys,
        values,
        far_rows,
        far_rows,
        o_weight,
        placed,
    )


def local(
    tile_cls,
    ln_gain,
    ln_bias,
    gate_weight,
    up_weight,
    down_weight,
    layer_scale,
    final_gain,
    final_bias,
    proj_weight,
    proj_bias,
    slot,
    slide_lengths,
    attn_gain,
    attn_bias,
    q_weight,
    k_weight,
    v_weight,
    o_weight,
):
    tile_rows = tile_cls.shape[0]
    width = proj_weight.shape[1]
    residual = tile_cls.astype(jnp.float32)
    normed = layer_norm(residual, ln_gain, ln_bias).astype(jnp.bfloat16)
    seq_index = lax.axis_index("seq")
    mlp_out = ffn_sums(normed, gate_weight, up_weight, down_weight)
    tile_out = residual + layer_scale * mlp_out
    final = layer_norm(tile_out, final_gain, final_bias).astype(jnp.bfloat16)
    embed = (jnp.dot(final, proj_weight, preferred_element_type=jnp.float32) + proj_bias).astype(
        jnp.bfloat16
    )
    devices = lax.axis_size("grp") * lax.axis_size("seq")
    capacity = 2 * tile_rows // devices
    target = slot // tile_rows
    position = slot % tile_rows
    order = jnp.arange(tile_rows, dtype=jnp.int32)
    same = (target[:, None] == target[None, :]) & (order[None, :] < order[:, None])
    bucket = target * capacity + jnp.sum(same.astype(jnp.int32), 1)
    places = jnp.arange(devices * capacity, dtype=jnp.int32)
    sends = places[:, None] == bucket[None, :]
    lane = jnp.arange(128, dtype=jnp.int32)[None, :]
    code = jnp.where(lane == 0, position[:, None] // 16, position[:, None] % 16)
    code = jnp.where(lane < 2, code, 0) + (lane == 2)
    tagged = jnp.concatenate([embed, code.astype(jnp.bfloat16)], 1)
    outgoing = (
        jnp.dot(sends.astype(jnp.bfloat16), tagged, preferred_element_type=jnp.float32)
        .astype(jnp.bfloat16)
        .reshape(devices, capacity, width + 128)
    )
    incoming = lax.all_to_all(outgoing, ("grp", "seq"), split_axis=0, concat_axis=0, tiled=True)
    incoming = incoming.reshape(-1, width + 128)
    arrived = incoming[:, :width]
    tags = incoming[:, width : width + 3].astype(jnp.int32)
    arrived_place = jnp.where(tags[:, 2] == 1, tags[:, 0] * 16 + tags[:, 1], tile_rows)
    lands = (order[:, None] == arrived_place[None, :]).astype(jnp.bfloat16)
    placed = jnp.dot(lands, arrived, preferred_element_type=jnp.float32).astype(jnp.bfloat16)
    slide_ends = jnp.cumsum(slide_lengths[0])

    seq_resid = placed.astype(jnp.float32)
    span = W_SEG // tile_rows
    normed_seq = layer_norm(seq_resid, attn_gain, attn_bias).astype(jnp.bfloat16)
    block = jnp.concatenate(
        [normed_seq] + [crossed(normed_seq, r) for r in range(1, span)], 0
    )
    queries = jnp.dot(normed_seq, q_weight, preferred_element_type=jnp.float32).astype(
        jnp.bfloat16
    )
    keys_proj = jnp.dot(block, k_weight, preferred_element_type=jnp.float32).astype(jnp.bfloat16)
    values_proj = jnp.dot(block, v_weight, preferred_element_type=jnp.float32).astype(
        jnp.bfloat16
    )
    chosen = jnp.concatenate([pick_dilated(keys_proj), pick_dilated(values_proj)], 1)
    far_pieces = [chosen] + [
        crossed(chosen, r) for r in range(span, lax.axis_size("seq"), span)
    ]
    far_rows = jnp.concatenate(far_pieces, 0)

    def spots(peers, step):
        offsets = jnp.arange(0, tile_rows, step, dtype=jnp.int32)
        return jnp.concatenate([(seq_index ^ r) * tile_rows + offsets for r in peers])

    result = attend(
        slide_ends,
        spots([0], 1)[:, None],
        spots(range(span), 1)[None, :],
        spots(range(lax.axis_size("seq")), RATE)[None, :],
        queries,
        keys_proj,
        values_proj,
        far_rows,
        o_weight,
        placed,
    )
    return result[None]


def solution(mesh):
    return jax.shard_map(
        local,
        mesh=mesh,
        in_specs=(
            P(("grp", "seq"), None),
            P(),
            P(),
            P("seq", None),
            P("seq", None),
            P("seq", None),
            P(),
            P(),
            P(),
            P(),
            P(),
            P(("grp", "seq")),
            P("grp", None),
            P(),
            P(),
            P(),
            P(),
            P(),
            P(),
        ),
        out_specs=P("grp", "seq", None),
        check_vma=False,
    )
```

```python
import functools

import jax
import jax.numpy as jnp
from jax import lax
from jax.experimental import pallas as pl
from jax.experimental.pallas import tpu as pltpu
from jax.sharding import PartitionSpec as P

HEADS = 12
HEAD_DIM = 64
W_SEG = 1024
RATE = 16


def crossed(block, offset):
    count = lax.axis_size("seq")
    return lax.ppermute(block, "seq", [(low, low ^ offset) for low in range(count)])


DEPTH = 4
SPOT = {1: 0, 3: 1, 2: 2, 0: 3}


def ffn_kernel(
    across,
    normed_ref,
    gate_ref,
    up_ref,
    down_ref,
    out_ref,
    tiles,
    weights,
    sums,
    right_out,
    left_out,
    right_in,
    left_in,
    local_sem,
    tile_send,
    tile_recv,
    y_send,
    y_recv,
    twin_send,
    twin_recv,
    right_send,
    right_recv,
    left_send,
    left_recv,
):
    seq = lax.axis_index("seq")
    grp = lax.axis_index("grp")
    z = seq // across
    y = seq % across
    core = grp % 2
    twin = grp + 1 - 2 * core
    has_right = z < DEPTH - 1
    has_left = z > 0
    rows = out_ref.shape[0]
    count = gate_ref.shape[0]
    half = count // 2
    own = (gate_ref, up_ref, down_ref)

    def y_peer(r):
        return {"seq": z * across + (y + r) % across}

    barrier = pltpu.get_barrier_semaphore()

    @pl.when(has_right)
    def _():
        pl.semaphore_signal(barrier, inc=1, device_id={"seq": seq + across})

    @pl.when(has_left)
    def _():
        pl.semaphore_signal(barrier, inc=1, device_id={"seq": seq - across})

    for r in range(1, across):
        pl.semaphore_signal(barrier, inc=1, device_id=y_peer(r))
    pl.semaphore_signal(barrier, inc=1, device_id={"grp": twin})

    loads = [pltpu.make_async_copy(normed_ref, tiles.at[SPOT[0]], local_sem.at[3])]
    loads += [
        pltpu.make_async_copy(own[i], weights.at[0, i], local_sem.at[i]) for i in range(3)
    ]
    for load in loads:
        load.start()
    pl.semaphore_wait(
        barrier,
        across + has_right.astype(jnp.int32) + has_left.astype(jnp.int32),
    )
    loads[0].wait()

    def hop_right(k):
        return pltpu.make_async_remote_copy(
            src_ref=tiles.at[SPOT[k - 1]],
            dst_ref=tiles.at[SPOT[k]],
            send_sem=tile_send.at[0, k - 1],
            recv_sem=tile_recv.at[k - 1],
            device_id={"seq": seq + across},
        )

    def hop_left(k):
        return pltpu.make_async_remote_copy(
            src_ref=tiles.at[SPOT[(DEPTH - k + 1) % DEPTH]],
            dst_ref=tiles.at[SPOT[DEPTH - k]],
            send_sem=tile_send.at[1, k - 1],
            recv_sem=tile_recv.at[DEPTH - k - 1],
            device_id={"seq": seq - across},
        )

    mine = pl.ds(pl.multiple_of(core * half, half), half)
    theirs = pl.ds(pl.multiple_of((1 - core) * half, half), half)

    def y_copy(r, i):
        return pltpu.make_async_remote_copy(
            src_ref=own[i].at[mine],
            dst_ref=weights.at[r, i, mine],
            send_sem=y_send.at[r, i],
            recv_sem=y_recv.at[r, i],
            device_id=y_peer(r),
        )

    def twin_copy(r, i, part):
        return pltpu.make_async_remote_copy(
            src_ref=weights.at[r, i, part],
            dst_ref=weights.at[r, i, part],
            send_sem=twin_send.at[r, i],
            recv_sem=twin_recv.at[r, i],
            device_id={"grp": twin},
        )

    @pl.when(has_right)
    def _():
        hop_right(1).start()

    @pl.when(has_left)
    def _():
        hop_left(1).start()

    fetches = [(r, i) for r in range(1, across) for i in range(3)]
    for r, i in fetches:
        y_copy(r, i).start()

    def relay(r, i):
        y_copy(r, i).wait_recv()
        twin_copy(r, i, mine).start()

    def products(spot_of, spot_count, low, high):
        def step(index, carry):
            spot = spot_of(index // (high - low))
            r = low + index % (high - low)
            tile = tiles[spot]
            dims = (((1,), (1,)), ((), ()))
            gate = lax.dot_general(
                tile, weights[r, 0], dims, preferred_element_type=jnp.float32
            )
            up_part = lax.dot_general(
                tile, weights[r, 1], dims, preferred_element_type=jnp.float32
            )
            hidden = (gate / (1.0 + jnp.exp(-gate)) * up_part).astype(jnp.bfloat16)
            term = jnp.dot(hidden, weights[r, 2], preferred_element_type=jnp.float32)

            @pl.when(r == 0)
            def _():
                sums[spot] = term

            @pl.when(r > 0)
            def _():
                sums[spot] += term

            return carry

        lax.fori_loop(0, spot_count * (high - low), step, 0)

    marks = [len(fetches) // 3, 2 * len(fetches) // 3]
    done = 0
    for k in range(1, DEPTH):

        @pl.when(z >= k)
        def _():
            hop_right(k).wait_recv()

        if k < DEPTH - 1:

            @pl.when((z >= k) & has_right)
            def _():
                hop_right(k + 1).start()

        @pl.when(z <= DEPTH - 1 - k)
        def _():
            hop_left(k).wait_recv()

        if k < DEPTH - 1:

            @pl.when((z <= DEPTH - 1 - k) & has_left)
            def _():
                hop_left(k + 1).start()

            while done < marks[k - 1]:
                relay(*fetches[done])
                done += 1
        if k == DEPTH - 2:
            for load in loads[1:]:
                load.wait()
            products(lambda j: 2 + j, 2, 0, 1)
    while done < len(fetches):
        relay(*fetches[done])
        done += 1
    for r, i in fetches:
        twin_copy(r, i, theirs).wait_recv()

    def sum_right(t):
        return pltpu.make_async_remote_copy(
            src_ref=right_out.at[t - 1],
            dst_ref=right_in.at[t - 1],
            send_sem=right_send.at[t - 1],
            recv_sem=right_recv.at[t - 1],
            device_id={"seq": seq + across},
        )

    def sum_left(t):
        return pltpu.make_async_remote_copy(
            src_ref=left_out.at[t - 1],
            dst_ref=left_in.at[t - 1],
            send_sem=left_send.at[t - 1],
            recv_sem=left_recv.at[t - 1],
            device_id={"seq": seq - across},
        )

    def pass_on(t):
        right_term, left_term = sums.at[SPOT[t]], sums.at[SPOT[DEPTH - t]]

        @pl.when(z == 0)
        def _():
            right_out[t - 1] = right_term[...].astype(jnp.bfloat16)

        @pl.when(z == DEPTH - 1)
        def _():
            left_out[t - 1] = left_term[...].astype(jnp.bfloat16)

        if t > 1:

            @pl.when((z >= 1) & (z <= t - 1))
            def _():
                sum_right(t - 1).wait_recv()
                right_out[t - 1] = (
                    right_term[...] + right_in[t - 2].astype(jnp.float32)
                ).astype(jnp.bfloat16)

        @pl.when((z <= t - 1) & has_right)
        def _():
            sum_right(t).start()

        if t > 1:

            @pl.when((z <= DEPTH - 2) & (z >= DEPTH - t))
            def _():
                sum_left(t - 1).wait_recv()
                left_out[t - 1] = (
                    left_term[...] + left_in[t - 2].astype(jnp.float32)
                ).astype(jnp.bfloat16)

        @pl.when((z >= DEPTH - t) & has_left)
        def _():
            sum_left(t).start()

    flip = (z >= DEPTH // 2).astype(jnp.int32)
    products(lambda j: flip, 1, 0, across)
    pass_on(1)
    products(lambda j: 2 + j, 2, 1, across)
    products(lambda j: 1 - flip, 1, 0, across)
    pass_on(2)
    pass_on(3)

    @pl.when(has_left)
    def _():
        sum_right(DEPTH - 1).wait_recv()
        sums[SPOT[0]] += right_in[DEPTH - 2].astype(jnp.float32)

    @pl.when(has_right)
    def _():
        sum_left(DEPTH - 1).wait_recv()
        sums[SPOT[0]] += left_in[DEPTH - 2].astype(jnp.float32)

    out_ref[...] = sums[SPOT[0]]

    for k in range(1, DEPTH):

        @pl.when((z >= k - 1) & has_right)
        def _():
            hop_right(k).wait_send()

        @pl.when((z <= DEPTH - k) & has_left)
        def _():
            hop_left(k).wait_send()

        @pl.when((z <= k - 1) & has_right)
        def _():
            sum_right(k).wait_send()

        @pl.when((z >= DEPTH - k) & has_left)
        def _():
            sum_left(k).wait_send()

    for r, i in fetches:
        y_copy(r, i).wait_send()
        twin_copy(r, i, mine).wait_send()


def ffn_sums(normed, gate_weight, up_weight, down_weight):
    across = lax.axis_size("seq") // DEPTH
    rows, width = normed.shape
    count = gate_weight.shape[0]
    messages = pltpu.VMEM((DEPTH - 1, rows, width), jnp.bfloat16)
    sem = pltpu.SemaphoreType.DMA
    flops = 6 * DEPTH * rows * across * count * width
    return pl.pallas_call(
        functools.partial(ffn_kernel, across),
        out_shape=jax.ShapeDtypeStruct((rows, width), jnp.float32),
        in_specs=[pl.BlockSpec(memory_space=pl.ANY)] * 4,
        out_specs=pl.BlockSpec(memory_space=pltpu.VMEM),
        scratch_shapes=[
            pltpu.VMEM((DEPTH, rows, width), jnp.bfloat16),
            pltpu.VMEM((across, 3, count, width), jnp.bfloat16),
            pltpu.VMEM((DEPTH, rows, width), jnp.float32),
            messages,
            messages,
            messages,
            messages,
            sem((4,)),
            sem((2, DEPTH - 1)),
            sem((DEPTH - 1,)),
            sem((across, 3)),
            sem((across, 3)),
            sem((across, 3)),
            sem((across, 3)),
            sem((DEPTH - 1,)),
            sem((DEPTH - 1,)),
            sem((DEPTH - 1,)),
            sem((DEPTH - 1,)),
        ],
        compiler_params=pltpu.CompilerParams(
            collective_id=0, has_side_effects=True, vmem_limit_bytes=48 << 20
        ),
        cost_estimate=pl.CostEstimate(
            flops=flops, bytes_accessed=6 * count * width, transcendentals=0
        ),
    )(normed, gate_weight, up_weight, down_weight)


def layer_norm(values, gain_vec, bias_vector):
    average = jnp.mean(values, -1, keepdims=True)
    centred = values - average
    variance = jnp.mean(centred * centred, -1, keepdims=True)
    return centred * lax.rsqrt(variance + 1e-06) * gain_vec + bias_vector


def pick_dilated(array):
    width = array.shape[1]
    grid = array.reshape(-1, RATE, width)
    own = jnp.arange(RATE)[:, None] == jnp.arange(width)[None, :] // HEAD_DIM
    return jnp.sum(jnp.where(own[None], grid, 0), 1, dtype=jnp.float32).astype(array.dtype)


def attention_kernel(
    ends_ref,
    query_pos_ref,
    key_pos_ref,
    far_pos_ref,
    query_ref,
    key_ref,
    value_ref,
    far_key_ref,
    far_value_ref,
    o_ref,
    resid_ref,
    out_ref,
    total,
):
    pair = pl.program_id(0)

    def slides(spots):
        return sum((spots >= ends_ref[j]).astype(jnp.int32) for j in range(ends_ref.shape[0]))

    @pl.when(pair == 0)
    def _():
        total[...] = resid_ref[...].astype(jnp.float32)

    query_pos = query_pos_ref[...]
    query_slide = slides(query_pos)
    near = query_slide == slides(key_pos_ref[...])
    query = query_ref[...] * HEAD_DIM ** (-0.5)
    lane = lax.broadcasted_iota(jnp.int32, query.shape, 1)
    dims = (((1,), (1,)), ((), ()))
    results = []
    for which in range(2):
        head = 2 * pair + which
        far = (query_slide == slides(far_pos_ref[...] + head)) & (query_pos % RATE == head)
        masked = jnp.where(lane // HEAD_DIM == which, query, jnp.zeros_like(query))
        scores = lax.dot_general(
            masked, key_ref[...], dims, preferred_element_type=jnp.float32
        )
        far_scores = lax.dot_general(
            masked, far_key_ref[...], dims, preferred_element_type=jnp.float32
        )
        scores = jnp.where(near, scores, -1e30)
        far_scores = jnp.where(far, far_scores, -1e30)
        peak = jnp.maximum(
            jnp.max(scores, -1, keepdims=True), jnp.max(far_scores, -1, keepdims=True)
        )
        share = jnp.exp(scores - peak)
        far_share = jnp.exp(far_scores - peak)
        weight = jnp.sum(share, -1, keepdims=True) + jnp.sum(far_share, -1, keepdims=True)
        mixed = jnp.dot(
            share.astype(jnp.bfloat16), value_ref[...], preferred_element_type=jnp.float32
        ) + jnp.dot(
            far_share.astype(jnp.bfloat16),
            far_value_ref[...],
            preferred_element_type=jnp.float32,
        )
        results.append(mixed / weight)
    attn = jnp.where(lane < HEAD_DIM, results[0], results[1]).astype(jnp.bfloat16)
    total[...] += jnp.dot(attn, o_ref[...], preferred_element_type=jnp.float32)

    @pl.when(pair == pl.num_programs(0) - 1)
    def _():
        out_ref[...] = total[...].astype(jnp.bfloat16)


def attend(ends, query_pos, key_pos, far_pos, queries, keys, values, far_rows, o_weight, placed):
    rows, width = placed.shape
    pairs = width // 128
    key_count, far_count = keys.shape[0], far_rows.shape[0]

    def whole(array):
        return pl.BlockSpec(array.shape, lambda j: (0, 0))

    def column(count, first=0):
        return pl.BlockSpec((count, 128), lambda j: (0, first + j))

    return pl.pallas_call(
        attention_kernel,
        out_shape=jax.ShapeDtypeStruct((rows, width), jnp.bfloat16),
        grid=(pairs,),
        in_specs=[
            pl.BlockSpec(memory_space=pltpu.SMEM),
            whole(query_pos),
            whole(key_pos),
            whole(far_pos),
            column(rows),
            column(key_count),
            column(key_count),
            column(far_count),
            column(far_count, pairs),
            pl.BlockSpec((128, width), lambda j: (j, 0)),
            whole(placed),
        ],
        out_specs=pl.BlockSpec((rows, width), lambda j: (0, 0)),
        scratch_shapes=[pltpu.VMEM((rows, width), jnp.float32)],
        compiler_params=pltpu.CompilerParams(
            dimension_semantics=("arbitrary",), vmem_limit_bytes=32 << 20
        ),
        cost_estimate=pl.CostEstimate(
            flops=8 * rows * (key_count + far_count) * width,
            bytes_accessed=4 * key_count * width,
            transcendentals=rows * (key_count + far_count) * HEADS,
        ),
    )(
        ends,
        query_pos,
        key_pos,
        far_pos,
        queries,
        keys,
        values,
        far_rows,
        far_rows,
        o_weight,
        placed,
    )


def local(
    tile_cls,
    ln_gain,
    ln_bias,
    gate_weight,
    up_weight,
    down_weight,
    layer_scale,
    final_gain,
    final_bias,
    proj_weight,
    proj_bias,
    slot,
    slide_lengths,
    attn_gain,
    attn_bias,
    q_weight,
    k_weight,
    v_weight,
    o_weight,
):
    tile_rows = tile_cls.shape[0]
    width = proj_weight.shape[1]
    residual = tile_cls.astype(jnp.float32)
    normed = layer_norm(residual, ln_gain, ln_bias).astype(jnp.bfloat16)
    seq_index = lax.axis_index("seq")
    mlp_out = ffn_sums(normed, gate_weight, up_weight, down_weight)
    tile_out = residual + layer_scale * mlp_out
    final = layer_norm(tile_out, final_gain, final_bias).astype(jnp.bfloat16)
    embed = (jnp.dot(final, proj_weight, preferred_element_type=jnp.float32) + proj_bias).astype(
        jnp.bfloat16
    )
    devices = lax.axis_size("grp") * lax.axis_size("seq")
    capacity = 2 * tile_rows // devices
    target = slot // tile_rows
    position = slot % tile_rows
    order = jnp.arange(tile_rows, dtype=jnp.int32)
    same = (target[:, None] == target[None, :]) & (order[None, :] < order[:, None])
    bucket = target * capacity + jnp.sum(same.astype(jnp.int32), 1)
    places = jnp.arange(devices * capacity, dtype=jnp.int32)
    sends = places[:, None] == bucket[None, :]
    lane = jnp.arange(128, dtype=jnp.int32)[None, :]
    code = jnp.where(lane == 0, position[:, None] // 16, position[:, None] % 16)
    code = jnp.where(lane < 2, code, 0) + (lane == 2)
    tagged = jnp.concatenate([embed, code.astype(jnp.bfloat16)], 1)
    outgoing = (
        jnp.dot(sends.astype(jnp.bfloat16), tagged, preferred_element_type=jnp.float32)
        .astype(jnp.bfloat16)
        .reshape(devices, capacity, width + 128)
    )
    incoming = lax.all_to_all(outgoing, ("grp", "seq"), split_axis=0, concat_axis=0, tiled=True)
    incoming = incoming.reshape(-1, width + 128)
    arrived = incoming[:, :width]
    tags = incoming[:, width : width + 3].astype(jnp.int32)
    arrived_place = jnp.where(tags[:, 2] == 1, tags[:, 0] * 16 + tags[:, 1], tile_rows)
    lands = (order[:, None] == arrived_place[None, :]).astype(jnp.bfloat16)
    placed = jnp.dot(lands, arrived, preferred_element_type=jnp.float32).astype(jnp.bfloat16)
    slide_ends = jnp.cumsum(slide_lengths[0])

    seq_resid = placed.astype(jnp.float32)
    span = W_SEG // tile_rows
    normed_seq = layer_norm(seq_resid, attn_gain, attn_bias).astype(jnp.bfloat16)
    chosen = jnp.concatenate(
        [
            pick_dilated(
                jnp.dot(normed_seq, weight, preferred_element_type=jnp.float32).astype(
                    jnp.bfloat16
                )
            )
            for weight in (k_weight, v_weight)
        ],
        1,
    )
    sent = [crossed(chosen, r) for r in range(span, lax.axis_size("seq"))]
    block = jnp.concatenate(
        [normed_seq] + [crossed(normed_seq, r) for r in range(1, span)], 0
    )
    queries = jnp.dot(normed_seq, q_weight, preferred_element_type=jnp.float32).astype(
        jnp.bfloat16
    )
    keys_proj = jnp.dot(block, k_weight, preferred_element_type=jnp.float32).astype(jnp.bfloat16)
    values_proj = jnp.dot(block, v_weight, preferred_element_type=jnp.float32).astype(
        jnp.bfloat16
    )
    near_chosen = jnp.concatenate([pick_dilated(keys_proj), pick_dilated(values_proj)], 1)
    far_pieces = [near_chosen] + sent
    far_rows = jnp.concatenate(far_pieces, 0)

    def spots(peers, step):
        offsets = jnp.arange(0, tile_rows, step, dtype=jnp.int32)
        return jnp.concatenate([(seq_index ^ r) * tile_rows + offsets for r in peers])

    result = attend(
        slide_ends,
        spots([0], 1)[:, None],
        spots(range(span), 1)[None, :],
        spots(range(lax.axis_size("seq")), RATE)[None, :],
        queries,
        keys_proj,
        values_proj,
        far_rows,
        o_weight,
        placed,
    )
    return result[None]


def solution(mesh):
    return jax.shard_map(
        local,
        mesh=mesh,
        in_specs=(
            P(("grp", "seq"), None),
            P(),
            P(),
            P("seq", None),
            P("seq", None),
            P("seq", None),
            P(),
            P(),
            P(),
            P(),
            P(),
            P(("grp", "seq")),
            P("grp", None),
            P(),
            P(),
            P(),
            P(),
            P(),
            P(),
        ),
        out_specs=P("grp", "seq", None),
        check_vma=False,
    )
```

```python
import functools

import jax
import jax.numpy as jnp
from jax import lax
from jax.experimental import pallas as pl
from jax.experimental.pallas import tpu as pltpu
from jax.sharding import PartitionSpec as P

HEADS = 12
HEAD_DIM = 64
W_SEG = 1024
RATE = 16


def crossed(block, offset):
    count = lax.axis_size("seq")
    return lax.ppermute(block, "seq", [(low, low ^ offset) for low in range(count)])


DEPTH = 4
SPOT = {1: 0, 3: 1, 2: 2, 0: 3}


def ffn_kernel(
    across,
    tile_ref,
    gain_ref,
    bias_ref,
    gate_ref,
    up_ref,
    down_ref,
    out_ref,
    tiles,
    weights,
    sums,
    right_out,
    left_out,
    right_in,
    left_in,
    local_sem,
    tile_send,
    tile_recv,
    y_send,
    y_recv,
    twin_send,
    twin_recv,
    right_send,
    right_recv,
    left_send,
    left_recv,
):
    seq = lax.axis_index("seq")
    grp = lax.axis_index("grp")
    z = seq // across
    y = seq % across
    core = grp % 2
    twin = grp + 1 - 2 * core
    has_right = z < DEPTH - 1
    has_left = z > 0
    rows = out_ref.shape[0]
    count = gate_ref.shape[0]
    half = count // 2
    own = (gate_ref, up_ref, down_ref)

    def y_peer(r):
        return {"seq": z * across + (y + r) % across}

    barrier = pltpu.get_barrier_semaphore()

    @pl.when(has_right)
    def _():
        pl.semaphore_signal(barrier, inc=1, device_id={"seq": seq + across})

    @pl.when(has_left)
    def _():
        pl.semaphore_signal(barrier, inc=1, device_id={"seq": seq - across})

    for r in range(1, across):
        pl.semaphore_signal(barrier, inc=1, device_id=y_peer(r))
    pl.semaphore_signal(barrier, inc=1, device_id={"grp": twin})

    loads = [
        pltpu.make_async_copy(own[i], weights.at[0, i], local_sem.at[i]) for i in range(3)
    ]
    for load in loads:
        load.start()
    tiles[SPOT[0]] = layer_norm(
        tile_ref[...].astype(jnp.float32), gain_ref[...], bias_ref[...]
    ).astype(jnp.bfloat16)
    pl.semaphore_wait(
        barrier,
        across + has_right.astype(jnp.int32) + has_left.astype(jnp.int32),
    )

    def hop_right(k):
        return pltpu.make_async_remote_copy(
            src_ref=tiles.at[SPOT[k - 1]],
            dst_ref=tiles.at[SPOT[k]],
            send_sem=tile_send.at[0, k - 1],
            recv_sem=tile_recv.at[k - 1],
            device_id={"seq": seq + across},
        )

    def hop_left(k):
        return pltpu.make_async_remote_copy(
            src_ref=tiles.at[SPOT[(DEPTH - k + 1) % DEPTH]],
            dst_ref=tiles.at[SPOT[DEPTH - k]],
            send_sem=tile_send.at[1, k - 1],
            recv_sem=tile_recv.at[DEPTH - k - 1],
            device_id={"seq": seq - across},
        )

    mine = pl.ds(pl.multiple_of(core * half, half), half)
    theirs = pl.ds(pl.multiple_of((1 - core) * half, half), half)

    def y_copy(r, i):
        return pltpu.make_async_remote_copy(
            src_ref=own[i].at[mine],
            dst_ref=weights.at[r, i, mine],
            send_sem=y_send.at[r, i],
            recv_sem=y_recv.at[r, i],
            device_id=y_peer(r),
        )

    def twin_copy(r, i, part):
        return pltpu.make_async_remote_copy(
            src_ref=weights.at[r, i, part],
            dst_ref=weights.at[r, i, part],
            send_sem=twin_send.at[r, i],
            recv_sem=twin_recv.at[r, i],
            device_id={"grp": twin},
        )

    @pl.when(has_right)
    def _():
        hop_right(1).start()

    @pl.when(has_left)
    def _():
        hop_left(1).start()

    fetches = [(r, i) for r in range(1, across) for i in range(3)]
    for r, i in fetches:
        y_copy(r, i).start()

    def relay(r, i):
        y_copy(r, i).wait_recv()
        twin_copy(r, i, mine).start()

    def products(spot_of, spot_count, low, high):
        def step(index, carry):
            spot = spot_of(index // (high - low))
            r = low + index % (high - low)
            tile = tiles[spot]
            dims = (((1,), (1,)), ((), ()))
            gate = lax.dot_general(
                tile, weights[r, 0], dims, preferred_element_type=jnp.float32
            )
            up_part = lax.dot_general(
                tile, weights[r, 1], dims, preferred_element_type=jnp.float32
            )
            hidden = (gate / (1.0 + jnp.exp(-gate)) * up_part).astype(jnp.bfloat16)
            term = jnp.dot(hidden, weights[r, 2], preferred_element_type=jnp.float32)

            @pl.when(r == 0)
            def _():
                sums[spot] = term

            @pl.when(r > 0)
            def _():
                sums[spot] += term

            return carry

        lax.fori_loop(0, spot_count * (high - low), step, 0)

    marks = [len(fetches) // 3, 2 * len(fetches) // 3]
    done = 0
    for k in range(1, DEPTH):

        @pl.when(z >= k)
        def _():
            hop_right(k).wait_recv()

        if k < DEPTH - 1:

            @pl.when((z >= k) & has_right)
            def _():
                hop_right(k + 1).start()

        @pl.when(z <= DEPTH - 1 - k)
        def _():
            hop_left(k).wait_recv()

        if k < DEPTH - 1:

            @pl.when((z <= DEPTH - 1 - k) & has_left)
            def _():
                hop_left(k + 1).start()

            while done < marks[k - 1]:
                relay(*fetches[done])
                done += 1
        if k == DEPTH - 2:
            for load in loads:
                load.wait()
            products(lambda j: 2 + j, 2, 0, 1)
    while done < len(fetches):
        relay(*fetches[done])
        done += 1
    for r, i in fetches:
        twin_copy(r, i, theirs).wait_recv()

    def sum_right(t):
        return pltpu.make_async_remote_copy(
            src_ref=right_out.at[t - 1],
            dst_ref=right_in.at[t - 1],
            send_sem=right_send.at[t - 1],
            recv_sem=right_recv.at[t - 1],
            device_id={"seq": seq + across},
        )

    def sum_left(t):
        return pltpu.make_async_remote_copy(
            src_ref=left_out.at[t - 1],
            dst_ref=left_in.at[t - 1],
            send_sem=left_send.at[t - 1],
            recv_sem=left_recv.at[t - 1],
            device_id={"seq": seq - across},
        )

    def pass_on(t):
        right_term, left_term = sums.at[SPOT[t]], sums.at[SPOT[DEPTH - t]]

        @pl.when(z == 0)
        def _():
            right_out[t - 1] = right_term[...].astype(jnp.bfloat16)

        @pl.when(z == DEPTH - 1)
        def _():
            left_out[t - 1] = left_term[...].astype(jnp.bfloat16)

        if t > 1:

            @pl.when((z >= 1) & (z <= t - 1))
            def _():
                sum_right(t - 1).wait_recv()
                right_out[t - 1] = (
                    right_term[...] + right_in[t - 2].astype(jnp.float32)
                ).astype(jnp.bfloat16)

        @pl.when((z <= t - 1) & has_right)
        def _():
            sum_right(t).start()

        if t > 1:

            @pl.when((z <= DEPTH - 2) & (z >= DEPTH - t))
            def _():
                sum_left(t - 1).wait_recv()
                left_out[t - 1] = (
                    left_term[...] + left_in[t - 2].astype(jnp.float32)
                ).astype(jnp.bfloat16)

        @pl.when((z >= DEPTH - t) & has_left)
        def _():
            sum_left(t).start()

    flip = (z >= DEPTH // 2).astype(jnp.int32)
    products(lambda j: flip, 1, 0, across)
    pass_on(1)
    products(lambda j: 2 + j, 2, 1, across)
    products(lambda j: 1 - flip, 1, 0, across)
    pass_on(2)
    pass_on(3)

    @pl.when(has_left)
    def _():
        sum_right(DEPTH - 1).wait_recv()
        sums[SPOT[0]] += right_in[DEPTH - 2].astype(jnp.float32)

    @pl.when(has_right)
    def _():
        sum_left(DEPTH - 1).wait_recv()
        sums[SPOT[0]] += left_in[DEPTH - 2].astype(jnp.float32)

    out_ref[...] = sums[SPOT[0]]

    for k in range(1, DEPTH):

        @pl.when((z >= k - 1) & has_right)
        def _():
            hop_right(k).wait_send()

        @pl.when((z <= DEPTH - k) & has_left)
        def _():
            hop_left(k).wait_send()

        @pl.when((z <= k - 1) & has_right)
        def _():
            sum_right(k).wait_send()

        @pl.when((z >= DEPTH - k) & has_left)
        def _():
            sum_left(k).wait_send()

    for r, i in fetches:
        y_copy(r, i).wait_send()
        twin_copy(r, i, mine).wait_send()


def ffn_sums(tile_cls, gain, bias, gate_weight, up_weight, down_weight):
    across = lax.axis_size("seq") // DEPTH
    rows, width = tile_cls.shape
    count = gate_weight.shape[0]
    messages = pltpu.VMEM((DEPTH - 1, rows, width), jnp.bfloat16)
    sem = pltpu.SemaphoreType.DMA
    flops = 6 * DEPTH * rows * across * count * width
    return pl.pallas_call(
        functools.partial(ffn_kernel, across),
        out_shape=jax.ShapeDtypeStruct((rows, width), jnp.float32),
        in_specs=[pl.BlockSpec(memory_space=pltpu.VMEM)] * 3
        + [pl.BlockSpec(memory_space=pl.ANY)] * 3,
        out_specs=pl.BlockSpec(memory_space=pltpu.VMEM),
        scratch_shapes=[
            pltpu.VMEM((DEPTH, rows, width), jnp.bfloat16),
            pltpu.VMEM((across, 3, count, width), jnp.bfloat16),
            pltpu.VMEM((DEPTH, rows, width), jnp.float32),
            messages,
            messages,
            messages,
            messages,
            sem((3,)),
            sem((2, DEPTH - 1)),
            sem((DEPTH - 1,)),
            sem((across, 3)),
            sem((across, 3)),
            sem((across, 3)),
            sem((across, 3)),
            sem((DEPTH - 1,)),
            sem((DEPTH - 1,)),
            sem((DEPTH - 1,)),
            sem((DEPTH - 1,)),
        ],
        compiler_params=pltpu.CompilerParams(
            collective_id=0, has_side_effects=True, vmem_limit_bytes=48 << 20
        ),
        cost_estimate=pl.CostEstimate(
            flops=flops, bytes_accessed=6 * count * width, transcendentals=0
        ),
    )(tile_cls, gain[None], bias[None], gate_weight, up_weight, down_weight)


def layer_norm(values, gain_vec, bias_vector):
    average = jnp.mean(values, -1, keepdims=True)
    centred = values - average
    variance = jnp.mean(centred * centred, -1, keepdims=True)
    return centred * lax.rsqrt(variance + 1e-06) * gain_vec + bias_vector


def pick_dilated(array):
    width = array.shape[1]
    grid = array.reshape(-1, RATE, width)
    own = jnp.arange(RATE)[:, None] == jnp.arange(width)[None, :] // HEAD_DIM
    return jnp.sum(jnp.where(own[None], grid, 0), 1, dtype=jnp.float32).astype(array.dtype)


def attention_kernel(
    ends_ref,
    query_pos_ref,
    key_pos_ref,
    far_pos_ref,
    query_ref,
    key_ref,
    value_ref,
    far_key_ref,
    far_value_ref,
    o_ref,
    resid_ref,
    out_ref,
    total,
):
    pair = pl.program_id(0)

    def slides(spots):
        return sum((spots >= ends_ref[j]).astype(jnp.int32) for j in range(ends_ref.shape[0]))

    @pl.when(pair == 0)
    def _():
        total[...] = resid_ref[...].astype(jnp.float32)

    query_pos = query_pos_ref[...]
    query_slide = slides(query_pos)
    near = query_slide == slides(key_pos_ref[...])
    query = query_ref[...] * HEAD_DIM ** (-0.5)
    lane = lax.broadcasted_iota(jnp.int32, query.shape, 1)
    dims = (((1,), (1,)), ((), ()))
    results = []
    for which in range(2):
        head = 2 * pair + which
        far = (query_slide == slides(far_pos_ref[...] + head)) & (query_pos % RATE == head)
        masked = jnp.where(lane // HEAD_DIM == which, query, jnp.zeros_like(query))
        scores = lax.dot_general(
            masked, key_ref[...], dims, preferred_element_type=jnp.float32
        )
        far_scores = lax.dot_general(
            masked, far_key_ref[...], dims, preferred_element_type=jnp.float32
        )
        scores = jnp.where(near, scores, -1e30)
        far_scores = jnp.where(far, far_scores, -1e30)
        peak = jnp.maximum(
            jnp.max(scores, -1, keepdims=True), jnp.max(far_scores, -1, keepdims=True)
        )
        share = jnp.exp(scores - peak)
        far_share = jnp.exp(far_scores - peak)
        weight = jnp.sum(share, -1, keepdims=True) + jnp.sum(far_share, -1, keepdims=True)
        mixed = jnp.dot(
            share.astype(jnp.bfloat16), value_ref[...], preferred_element_type=jnp.float32
        ) + jnp.dot(
            far_share.astype(jnp.bfloat16),
            far_value_ref[...],
            preferred_element_type=jnp.float32,
        )
        results.append(mixed / weight)
    attn = jnp.where(lane < HEAD_DIM, results[0], results[1]).astype(jnp.bfloat16)
    total[...] += jnp.dot(attn, o_ref[...], preferred_element_type=jnp.float32)

    @pl.when(pair == pl.num_programs(0) - 1)
    def _():
        out_ref[...] = total[...].astype(jnp.bfloat16)


def attend(ends, query_pos, key_pos, far_pos, queries, keys, values, far_rows, o_weight, placed):
    rows, width = placed.shape
    pairs = width // 128
    key_count, far_count = keys.shape[0], far_rows.shape[0]

    def whole(array):
        return pl.BlockSpec(array.shape, lambda j: (0, 0))

    def column(count, first=0):
        return pl.BlockSpec((count, 128), lambda j: (0, first + j))

    return pl.pallas_call(
        attention_kernel,
        out_shape=jax.ShapeDtypeStruct((rows, width), jnp.bfloat16),
        grid=(pairs,),
        in_specs=[
            pl.BlockSpec(memory_space=pltpu.SMEM),
            whole(query_pos),
            whole(key_pos),
            whole(far_pos),
            column(rows),
            column(key_count),
            column(key_count),
            column(far_count),
            column(far_count, pairs),
            pl.BlockSpec((128, width), lambda j: (j, 0)),
            whole(placed),
        ],
        out_specs=pl.BlockSpec((rows, width), lambda j: (0, 0)),
        scratch_shapes=[pltpu.VMEM((rows, width), jnp.float32)],
        compiler_params=pltpu.CompilerParams(
            dimension_semantics=("arbitrary",), vmem_limit_bytes=32 << 20
        ),
        cost_estimate=pl.CostEstimate(
            flops=8 * rows * (key_count + far_count) * width,
            bytes_accessed=4 * key_count * width,
            transcendentals=rows * (key_count + far_count) * HEADS,
        ),
    )(
        ends,
        query_pos,
        key_pos,
        far_pos,
        queries,
        keys,
        values,
        far_rows,
        far_rows,
        o_weight,
        placed,
    )


def local(
    tile_cls,
    ln_gain,
    ln_bias,
    gate_weight,
    up_weight,
    down_weight,
    layer_scale,
    final_gain,
    final_bias,
    proj_weight,
    proj_bias,
    slot,
    slide_lengths,
    attn_gain,
    attn_bias,
    q_weight,
    k_weight,
    v_weight,
    o_weight,
):
    tile_rows = tile_cls.shape[0]
    width = proj_weight.shape[1]
    residual = tile_cls.astype(jnp.float32)
    seq_index = lax.axis_index("seq")
    mlp_out = ffn_sums(tile_cls, ln_gain, ln_bias, gate_weight, up_weight, down_weight)
    tile_out = residual + layer_scale * mlp_out
    final = layer_norm(tile_out, final_gain, final_bias).astype(jnp.bfloat16)
    embed = (jnp.dot(final, proj_weight, preferred_element_type=jnp.float32) + proj_bias).astype(
        jnp.bfloat16
    )
    devices = lax.axis_size("grp") * lax.axis_size("seq")
    capacity = 2 * tile_rows // devices
    target = slot // tile_rows
    position = slot % tile_rows
    order = jnp.arange(tile_rows, dtype=jnp.int32)
    same = (target[:, None] == target[None, :]) & (order[None, :] < order[:, None])
    bucket = target * capacity + jnp.sum(same.astype(jnp.int32), 1)
    places = jnp.arange(devices * capacity, dtype=jnp.int32)
    sends = places[:, None] == bucket[None, :]
    lane = jnp.arange(128, dtype=jnp.int32)[None, :]
    code = jnp.where(lane == 0, position[:, None] // 16, position[:, None] % 16)
    code = jnp.where(lane < 2, code, 0) + (lane == 2)
    tagged = jnp.concatenate([embed, code.astype(jnp.bfloat16)], 1)
    outgoing = (
        jnp.dot(sends.astype(jnp.bfloat16), tagged, preferred_element_type=jnp.float32)
        .astype(jnp.bfloat16)
        .reshape(devices, capacity, width + 128)
    )
    incoming = lax.all_to_all(outgoing, ("grp", "seq"), split_axis=0, concat_axis=0, tiled=True)
    incoming = incoming.reshape(-1, width + 128)
    arrived = incoming[:, :width]
    tags = incoming[:, width : width + 3].astype(jnp.int32)
    arrived_place = jnp.where(tags[:, 2] == 1, tags[:, 0] * 16 + tags[:, 1], tile_rows)
    lands = (order[:, None] == arrived_place[None, :]).astype(jnp.bfloat16)
    placed = jnp.dot(lands, arrived, preferred_element_type=jnp.float32).astype(jnp.bfloat16)
    slide_ends = jnp.cumsum(slide_lengths[0])

    seq_resid = placed.astype(jnp.float32)
    span = W_SEG // tile_rows
    normed_seq = layer_norm(seq_resid, attn_gain, attn_bias).astype(jnp.bfloat16)
    chosen = jnp.concatenate(
        [
            pick_dilated(
                jnp.dot(normed_seq, weight, preferred_element_type=jnp.float32).astype(
                    jnp.bfloat16
                )
            )
            for weight in (k_weight, v_weight)
        ],
        1,
    )
    sent = [crossed(chosen, r) for r in range(span, lax.axis_size("seq"))]
    block = jnp.concatenate(
        [normed_seq] + [crossed(normed_seq, r) for r in range(1, span)], 0
    )
    queries = jnp.dot(normed_seq, q_weight, preferred_element_type=jnp.float32).astype(
        jnp.bfloat16
    )
    keys_proj = jnp.dot(block, k_weight, preferred_element_type=jnp.float32).astype(jnp.bfloat16)
    values_proj = jnp.dot(block, v_weight, preferred_element_type=jnp.float32).astype(
        jnp.bfloat16
    )
    near_chosen = jnp.concatenate([pick_dilated(keys_proj), pick_dilated(values_proj)], 1)
    far_pieces = [near_chosen] + sent
    far_rows = jnp.concatenate(far_pieces, 0)

    def spots(peers, step):
        offsets = jnp.arange(0, tile_rows, step, dtype=jnp.int32)
        return jnp.concatenate([(seq_index ^ r) * tile_rows + offsets for r in peers])

    result = attend(
        slide_ends,
        spots([0], 1)[:, None],
        spots(range(span), 1)[None, :],
        spots(range(lax.axis_size("seq")), RATE)[None, :],
        queries,
        keys_proj,
        values_proj,
        far_rows,
        o_weight,
        placed,
    )
    return result[None]


def solution(mesh):
    return jax.shard_map(
        local,
        mesh=mesh,
        in_specs=(
            P(("grp", "seq"), None),
            P(),
            P(),
            P("seq", None),
            P("seq", None),
            P("seq", None),
            P(),
            P(),
            P(),
            P(),
            P(),
            P(("grp", "seq")),
            P("grp", None),
            P(),
            P(),
            P(),
            P(),
            P(),
            P(),
        ),
        out_specs=P("grp", "seq", None),
        check_vma=False,
    )
```
